256 devices in a mesh: ep: 64 (over y, z, core), fs: 4 (over x).
Axes of the slice: x: 4, y: 4, z: 8, core: 2. Of those that a mesh axis runs over, the one named last changes fastest.
Arguments:
- tokens: bfloat16 [8192, 4096], P('ep', 'fs'), may hold values from -6 to 6
- grad_out: bfloat16 [8192, 4096], P('ep', 'fs'), may hold values from -6 to 6
- gate_weight: bfloat16 [4, 14336, 4096], P('fs', 'ep'), may hold values from -0.09375 to 0.09375
- up_weight: bfloat16 [4, 14336, 4096], P('fs', 'ep'), may hold values from -0.09375 to 0.09375
- down_weight: bfloat16 [4, 14336, 4096], P('fs', 'ep'), may hold values from -0.046875 to 0.046875
- gate_values: float32 [4, 256], P('fs'), may hold values from 0.25 to 1
- chosen: int32 [4, 256], replicated, may hold values from 0 to 8191, as said below
- counts: int32 [4], replicated, may hold values from 128 to 256, as said below
Outputs:
- gate_grad: bfloat16 [4, 14336, 4096], P('fs', 'ep')
- up_grad: bfloat16 [4, 14336, 4096], P('fs', 'ep')
- down_grad: bfloat16 [4, 14336, 4096], P('fs', 'ep')
- token_grad: bfloat16 [8192, 4096], P('ep', 'fs')
- score_grad: float32 [4, 256], P('fs')
The draws below stay inside these ranges and needn't reach their ends.
Inputs may be any that keep to these rules, and one draw needn't show every extreme that they name: `chosen`: the 256 entries of one row are distinct tokens; only the first counts[e] entries of row e are live, the others are padding to be ignored. Among the live entries of one expert at most 6 lie in one aligned block of 128 tokens (the tokens of one index of ep), and in every draw every expert has exactly 6 live entries in some block. `counts`: some expert has all 256 entries live in every draw.
All inputs are finite; a program needn't handle non-finite values.
Results may differ from the reference program's by a relative error of at most 0.0057.
Values may be sent and summed in bfloat16 or wider, within the bound.
No kernel may reach another device: no remote copies, remote signals or barrier semaphores. Data moves between devices by JAX's collectives and lax.ppermute only.
A program may use at most 128 MiB of HBM per device.

```python
import jax
import jax.numpy as jnp
from jax import lax

D = 4096
FF = 14336
EXPERTS = 4
TOK_EP = 128
TOKENS = 8192
CAP = 256
SLOTS = 6


def expert_routes(key):
    keys = jax.random.split(jax.random.fold_in(key, 7), 5)
    ep_count = TOKENS // TOK_EP
    pool = ep_count * SLOTS
    token_iota = lax.broadcasted_iota(jnp.int32, (EXPERTS, ep_count, TOK_EP), 2)
    scores = jax.random.randint(keys[0], (EXPERTS, ep_count, TOK_EP), 0, 1 << 16) * TOK_EP + token_iota
    order = jnp.argsort(scores, axis=2)[:, :, :SLOTS].astype(jnp.int32)
    block_base = lax.broadcasted_iota(jnp.int32, (EXPERTS, ep_count, SLOTS), 1)
    candidates = (order + block_base * TOK_EP).reshape(EXPERTS, pool)
    candidate_block = block_base.reshape(EXPERTS, pool)
    forced_block = jax.random.randint(keys[1], (EXPERTS, 1), 0, ep_count)
    pool_iota = lax.broadcasted_iota(jnp.int32, (EXPERTS, pool), 1)
    priority = jax.random.randint(keys[2], (EXPERTS, pool), 0, 1 << 16) * pool + pool_iota
    priority = jnp.where(candidate_block == forced_block, priority + (1 << 16) * pool, priority)
    ranked = jnp.argsort(-priority, axis=1)[:, :CAP].astype(jnp.int32)
    chosen = jnp.take_along_axis(candidates, ranked, axis=1)
    counts = jax.random.randint(keys[3], (EXPERTS,), CAP // 2, CAP + 1)
    full_expert = jax.random.randint(keys[4], (), 0, EXPERTS)
    counts = jnp.where(jnp.arange(EXPERTS) == full_expert, CAP, counts).astype(jnp.int32)
    return (chosen, counts)


def draw_chosen(key, part):
    return expert_routes(key)[0]


def draw_counts(key, part):
    return expert_routes(key)[1]


def block_levels(stream_key, extent, cuts, least, high):
    gain = 1.0
    for position, blocks in cuts:
        draws = jax.random.uniform(jax.random.fold_in(jax.random.fold_in(stream_key, 6), position), (blocks,), jnp.float32, least / len(cuts), high / len(cuts))
        gain = gain * jnp.repeat(jnp.exp(draws), extent[position] // blocks).reshape((-1,) + (1,) * (len(extent) - 1 - position))
    return gain


def bell_draw(stream_key, shape, spread, reach, shards=(), held_as=jnp.bfloat16):
    loudness = block_levels(stream_key, shape, shards, -0.22, 0.18) if shards else 1.0
    entries = jax.random.normal(stream_key, shape, jnp.float32) * spread * loudness
    return jnp.minimum(jnp.maximum(entries, -reach), reach).astype(held_as)


def setup_inputs(seed: int = 0) -> dict:
    splits = jax.random.split(jax.random.key(seed), 9)
    return {
        "tokens": bell_draw(splits[0], (TOKENS, D), 1.0, 6.0, ((0, 64), (1, 4))),
        "grad_out": bell_draw(splits[1], (TOKENS, D), 1.0, 6.0, ((0, 64), (1, 4))),
        "gate_weight": bell_draw(splits[2], (EXPERTS, FF, D), D ** -0.5, 0.09375, ((0, 4), (1, 64))),
        "up_weight": bell_draw(splits[3], (EXPERTS, FF, D), D ** -0.5, 0.09375, ((0, 4), (1, 64))),
        "down_weight": bell_draw(splits[4], (EXPERTS, FF, D), FF ** -0.5, 0.046875, ((0, 4), (1, 64))),
        "gate_values": jnp.clip(0.25 + 0.75 * jax.random.uniform(splits[5], (EXPERTS, CAP), jnp.float32) ** block_levels(splits[5], (EXPERTS, CAP), ((0, 4),), -0.2, 0.2), 0.25, 1.0),
        "chosen": draw_chosen(jax.random.fold_in(splits[8], 71), 0),
        "counts": draw_counts(jax.random.fold_in(splits[8], 71), 0),
    }


def expert_pass(x_rows, dy_rows, gate_rows, gate_w, up_w, down_w):
    pre_gate = jnp.dot(x_rows, gate_w.T, preferred_element_type=jnp.float32)
    pre_up = jnp.dot(x_rows, up_w.T, preferred_element_type=jnp.float32)
    sigmoid_val = jax.nn.sigmoid(pre_gate)
    swished = pre_gate * sigmoid_val
    active = (swished * pre_up).astype(jnp.bfloat16)
    probes = jnp.dot(dy_rows, down_w.T, preferred_element_type=jnp.float32)
    score_term = jnp.sum(active.astype(jnp.float32) * probes, axis=1)
    weighted = (gate_rows[:, None] * dy_rows.astype(jnp.float32)).astype(jnp.bfloat16)
    d_active = gate_rows[:, None] * probes
    d_gate = (d_active * pre_up * sigmoid_val * (1.0 + pre_gate * (1.0 - sigmoid_val))).astype(jnp.bfloat16)
    d_up = (d_active * swished).astype(jnp.bfloat16)
    grad_g = jnp.dot(d_gate.T, x_rows, preferred_element_type=jnp.float32)
    grad_u = jnp.dot(d_up.T, x_rows, preferred_element_type=jnp.float32)
    grad_d = jnp.dot(active.T, weighted, preferred_element_type=jnp.float32)
    row_grad = jnp.dot(d_gate, gate_w, preferred_element_type=jnp.float32) + jnp.dot(d_up, up_w, preferred_element_type=jnp.float32)
    return grad_g, grad_u, grad_d, score_term, row_grad


def reference(tokens, grad_out, gate_weight, up_weight, down_weight, gate_values, chosen, counts):
    live = jnp.arange(CAP).astype(jnp.int32)[None, :] < counts[:, None]

    def one_expert(operands):
        index_row, live_row, gate_row, gate_w, up_w, down_w = operands
        zero_val = jnp.zeros((), tokens.dtype)
        x_rows = jnp.where(live_row[:, None], tokens[index_row], zero_val)
        dy_rows = jnp.where(live_row[:, None], grad_out[index_row], zero_val)
        grad_g, grad_u, grad_d, score_term, row_grad = expert_pass(x_rows, dy_rows, gate_row, gate_w, up_w, down_w)
        return (grad_g.astype(jnp.bfloat16), grad_u.astype(jnp.bfloat16), grad_d.astype(jnp.bfloat16), score_term, row_grad)

    gate_grad, up_grad, down_grad, score_grad, row_grads = lax.map(
        one_expert, (chosen, live, gate_values, gate_weight, up_weight, down_weight))
    flat_index = chosen.reshape(-1)
    summed = jnp.zeros((TOKENS, D), jnp.float32).at[flat_index].add(row_grads.reshape(-1, D))
    token_grad = summed.astype(jnp.bfloat16)
    return gate_grad, up_grad, down_grad, token_grad, score_grad
```

```python
import jax
import jax.numpy as jnp
from jax import lax
from jax.sharding import Mesh
from jax.sharding import PartitionSpec as P

SLOTS = 6
NY, NZ, NC, NX = 4, 8, 2, 4
BF, F32 = jnp.bfloat16, jnp.float32


def shift(n, s):
    return [(i, (i + s) % n) for i in range(n)]


def swap(v):
    return lax.ppermute(v, "c", [(0, 1), (1, 0)])


def butterfly(v):
    for axis, n in (("c", NC), ("y", NY), ("z", NZ)):
        step = 1
        while step < n:
            v = v + lax.ppermute(v, axis, [(i, i ^ step) for i in range(n)])
            step *= 2
    return v


def picks(tokens, grad_out, chosen, counts, ep):
    cap = chosen.shape[1]
    tok_rows = tokens.shape[0]
    col = lax.broadcasted_iota(jnp.int32, chosen.shape, 1)
    mine = (col < counts[:, None]) & (chosen // tok_rows == ep)
    before = lax.broadcasted_iota(jnp.int32, (cap, cap), 0) < lax.broadcasted_iota(
        jnp.int32, (cap, cap), 1
    )
    rank = jnp.dot(mine.astype(BF), before.astype(BF), preferred_element_type=F32).astype(jnp.int32)
    slot = lax.broadcasted_iota(jnp.int32, (1, SLOTS, 1), 1)
    hit = mine[:, None, :] & (rank[:, None, :] == slot)
    row = jnp.sum(jnp.where(hit, (chosen - ep * tok_rows)[:, None, :] + 1, 0), axis=2) - 1
    row = row.reshape(-1)
    onehot = (row[:, None] == lax.broadcasted_iota(jnp.int32, (1, tok_rows), 1)).astype(BF)
    px = jnp.dot(onehot, tokens, preferred_element_type=F32).astype(BF)
    pd = jnp.dot(onehot, grad_out, preferred_element_type=F32).astype(BF)
    return onehot, px, pd


def slot_table(chosen_e, count_e, tok_rows, total):
    cap = chosen_e.shape[0]
    col = lax.broadcasted_iota(jnp.int32, (cap,), 0)
    live = col < count_e
    block = jnp.where(live, chosen_e // tok_rows, -1)
    same = (block[:, None] == block[None, :]) & (col[:, None] < col[None, :])
    rank = jnp.sum(same.astype(jnp.int32), axis=0)
    pos = jnp.where(live, block * SLOTS + rank, total)
    return pos == lax.broadcasted_iota(jnp.int32, (total, cap), 0)


def on_device(tokens, grad_out, gate_weight, up_weight, down_weight, gate_values, chosen, counts):
    y = lax.axis_index("y")
    z = lax.axis_index("z")
    c = lax.axis_index("c")
    x = lax.axis_index("x")
    ep = (y * NZ + z) * NC + c
    tok_rows, quarter = tokens.shape
    experts = chosen.shape[0]
    total = NY * NZ * NC * SLOTS
    part = quarter // NC
    half = NX * part
    gw, uw, dw = gate_weight[0], up_weight[0], down_weight[0]
    hid = gw.shape[0]

    onehot, px, pd = picks(tokens, grad_out, chosen, counts, ep)
    send = jnp.stack([px, pd], 0).reshape(2, experts, SLOTS, NC, part)
    send = send.transpose(3, 1, 0, 2, 4).reshape(NC * experts, 2 * SLOTS, part)
    got = lax.all_to_all(send, ("c", "x"), 0, 0, tiled=True)
    got = got.reshape(NC, NX, 2, SLOTS, part).transpose(2, 0, 3, 1, 4).reshape(2, NC * SLOTS, half)
    x_own, d_own = got[0], got[1]

    nrow = NC * SLOTS
    x_line = lax.all_to_all(
        jnp.broadcast_to(x_own[None], (NZ, nrow, half)), "z", 0, 0, tiled=True
    ).reshape(NZ * nrow, half)
    d_line = lax.all_to_all(
        jnp.broadcast_to(d_own[None], (NY, nrow, half)), "y", 0, 0, tiled=True
    ).reshape(NY * nrow, half)

    xs = [x_line, None, None, None]
    xs[3] = lax.ppermute(x_line, "y", shift(NY, 1))
    xs[1] = lax.ppermute(x_line, "y", shift(NY, -1))
    hr = NZ * nrow // 2
    o1 = lax.ppermute(xs[3][:hr], "y", shift(NY, 1))
    o2 = lax.ppermute(xs[1][hr:], "y", shift(NY, -1))
    xs[2] = jnp.concatenate([o1, o2], 0)

    ds = [d_line] + [None] * 7
    up, dn = d_line, d_line
    for k in range(1, 4):
        up = lax.ppermute(up, "z", shift(NZ, 1))
        dn = lax.ppermute(dn, "z", shift(NZ, -1))
        ds[NZ - k] = up
        ds[k] = dn
    hd = NY * nrow // 2
    o1 = lax.ppermute(up[:hd], "z", shift(NZ, 1))
    o2 = lax.ppermute(dn[hd:], "z", shift(NZ, -1))
    ds[4] = jnp.concatenate([o1, o2], 0)

    def whole(parts, pos, n):
        mine = jnp.concatenate(parts, 0)
        other = swap(mine)
        pair = [jnp.where(c == 0, mine, other), jnp.where(c == 0, other, mine)]
        rows = mine.shape[0]
        v = jnp.stack([p.reshape(rows, NX, part) for p in pair], 2).reshape(rows, NX * quarter)
        v = v.reshape(n, rows // n, NX * quarter)
        v = jnp.concatenate([v, v], 0)
        return lax.dynamic_slice_in_dim(v, (n - pos) % n, n, 0).reshape(rows, NX * quarter)

    x_rows = whole(xs, y, NY)
    dy_rows = whole(ds, z, NZ)

    hits = slot_table(lax.dynamic_index_in_dim(chosen, x, 0, keepdims=False),
                      lax.dynamic_index_in_dim(counts, x, 0, keepdims=False), tok_rows, total)
    gate_x = jnp.sum(jnp.where(hits, gate_values[0][None, :], 0.0), axis=1)

    def to_dy(v):
        return v.reshape(NY, NZ, nrow, -1).transpose(1, 0, 2, 3).reshape(total, -1)

    def to_x(v):
        return v.reshape(NZ, NY, nrow, -1).transpose(1, 0, 2, 3).reshape(total, -1)

    gate_d = to_dy(gate_x[:, None])[:, 0]
    nt = (((1,), (1,)), ((), ()))
    pre_gate = lax.dot_general(x_rows, gw, nt, preferred_element_type=F32)
    pre_up = lax.dot_general(x_rows, uw, nt, preferred_element_type=F32)
    probe = to_x(lax.dot_general(dy_rows, dw, nt, preferred_element_type=F32))
    sig = jax.nn.sigmoid(pre_gate)
    swished = pre_gate * sig
    active = (swished * pre_up).astype(BF)
    score = jnp.sum(active.astype(F32) * probe, axis=1)
    d_active = gate_x[:, None] * probe
    d_gate = (d_active * pre_up * sig * (1.0 + pre_gate * (1.0 - sig))).astype(BF)
    d_up = (d_active * swished).astype(BF)
    weighted = (gate_d[:, None] * dy_rows.astype(F32)).astype(BF)

    d_both = jnp.concatenate([d_gate, d_up], 1)
    d_both_d = to_dy(d_both)
    w_both = jnp.concatenate([gw, uw], 0).reshape(2 * hid, NX, NC, part)
    w_mine = lax.dynamic_index_in_dim(w_both, c, 2, keepdims=False).reshape(2 * hid, half)
    w_other = lax.dynamic_index_in_dim(w_both, 1 - c, 2, keepdims=False).reshape(2 * hid, half)
    ha = half // 2

    def rows_of(w):
        a = jnp.dot(d_both, w[:, :ha], preferred_element_type=F32)
        b = jnp.dot(d_both_d, w[:, ha:], preferred_element_type=F32)
        return a, b

    oa, ob = rows_of(w_other)
    oa, ob = swap(oa.astype(BF)), swap(ob.astype(BF))
    ra, rb = rows_of(w_mine)
    ra = (ra + oa.astype(F32)).astype(BF)
    rb = (rb + ob.astype(F32)).astype(BF)
    a1 = lax.all_to_all(ra.reshape(NY, NZ * nrow, ha), "y", 0, 0, tiled=True)
    b1 = lax.all_to_all(rb.reshape(NZ, NY * nrow, ha), "z", 0, 0, tiled=True)
    a1 = jnp.sum(a1.astype(F32), 0).astype(BF)
    b1 = jnp.sum(b1.astype(F32), 0).astype(BF)
    a2 = lax.all_to_all(a1.reshape(NZ, nrow, ha), "z", 0, 0, tiled=True)
    b2 = lax.all_to_all(b1.reshape(NY, nrow, ha), "y", 0, 0, tiled=True)
    a2 = jnp.sum(a2.astype(F32), 0)
    b2 = jnp.sum(b2.astype(F32), 0)
    mine_rows = jnp.concatenate([a2, b2], 1)
    back = mine_rows.reshape(NC, SLOTS, NX, part).transpose(0, 2, 1, 3).reshape(NC * NX, SLOTS, part)
    back = lax.all_to_all(back, ("c", "x"), 0, 0, tiled=True)
    back = back.reshape(NC, experts, SLOTS, part).transpose(1, 2, 0, 3).reshape(experts * SLOTS, quarter)
    tn = (((0,), (0,)), ((), ()))
    token_grad = lax.dot_general(
        onehot.astype(F32), back, tn, precision=lax.Precision.HIGHEST, preferred_element_type=F32
    ).astype(BF)

    grad_g = lax.dot_general(d_gate, x_rows, tn, preferred_element_type=F32).astype(BF)
    grad_u = lax.dot_general(d_up, x_rows, tn, preferred_element_type=F32).astype(BF)
    grad_d = lax.dot_general(to_dy(active), weighted, tn, preferred_element_type=F32).astype(BF)
    score_sum = butterfly(score)
    score_grad = jnp.sum(jnp.where(hits, score_sum[:, None], 0.0), axis=0)
    return grad_g[None], grad_u[None], grad_d[None], token_grad, score_grad[None]


def solution(mesh):
    torus = Mesh(mesh.devices.reshape(NY, NZ, NC, NX), ("y", "z", "c", "x"))
    ep = ("y", "z", "c")
    return jax.shard_map(
        on_device,
        mesh=torus,
        in_specs=(
            P(ep, "x"),
            P(ep, "x"),
            P("x", ep, None),
            P("x", ep, None),
            P("x", ep, None),
            P("x", None),
            P(),
            P(),
        ),
        out_specs=(
            P("x", ep, None),
            P("x", ep, None),
            P("x", ep, None),
            P(ep, "x"),
            P("x", None),
        ),
        check_vma=False,
    )
```

```python
import jax
import jax.numpy as jnp
from jax import lax
from jax.experimental import pallas as pl
from jax.experimental.pallas import tpu as pltpu
from jax.sharding import Mesh
from jax.sharding import PartitionSpec as P

SLOTS = 6
NY, NZ, NC, NX = 4, 8, 2, 4
BF, F32 = jnp.bfloat16, jnp.float32
INTERPRET = False


def shift(n, s):
    return [(i, (i + s) % n) for i in range(n)]


def swap(v):
    return lax.ppermute(v, "c", [(0, 1), (1, 0)])


def butterfly(v):
    for axis, n in (("c", NC), ("y", NY), ("z", NZ)):
        step = 1
        while step < n:
            v = v + lax.ppermute(v, axis, [(i, i ^ step) for i in range(n)])
            step *= 2
    return v


def picks(tokens, grad_out, chosen, counts, ep):
    cap = chosen.shape[1]
    tok_rows = tokens.shape[0]
    col = lax.broadcasted_iota(jnp.int32, chosen.shape, 1)
    mine = (col < counts[:, None]) & (chosen // tok_rows == ep)
    before = lax.broadcasted_iota(jnp.int32, (cap, cap), 0) < lax.broadcasted_iota(
        jnp.int32, (cap, cap), 1
    )
    rank = jnp.dot(mine.astype(BF), before.astype(BF), preferred_element_type=F32).astype(jnp.int32)
    slot = lax.broadcasted_iota(jnp.int32, (1, SLOTS, 1), 1)
    hit = mine[:, None, :] & (rank[:, None, :] == slot)
    row = jnp.sum(jnp.where(hit, (chosen - ep * tok_rows)[:, None, :] + 1, 0), axis=2) - 1
    row = row.reshape(-1)
    onehot = (row[:, None] == lax.broadcasted_iota(jnp.int32, (1, tok_rows), 1)).astype(BF)
    px = jnp.dot(onehot, tokens, preferred_element_type=F32).astype(BF)
    pd = jnp.dot(onehot, grad_out, preferred_element_type=F32).astype(BF)
    return onehot, px, pd


def slot_table(chosen_e, count_e, tok_rows, total):
    cap = chosen_e.shape[0]
    col = lax.broadcasted_iota(jnp.int32, (cap,), 0)
    live = col < count_e
    block = jnp.where(live, chosen_e // tok_rows, -1)
    same = (block[:, None] == block[None, :]) & (col[:, None] < col[None, :])
    rank = jnp.sum(same.astype(jnp.int32), axis=0)
    pos = jnp.where(live, block * SLOTS + rank, total)
    return pos == lax.broadcasted_iota(jnp.int32, (total, cap), 0)


NT = (((1,), (1,)), ((), ()))
X_PARTS = (((0, 0, 0, 96),), ((0, 3, 0, 96),), ((0, 1, 0, 96),), ((0, 2, 0, 96),))
D_PARTS = (
    ((0, 0, 0, 48),),
    ((0, 7, 0, 48), (48, 1, 0, 48)),
    ((0, 6, 0, 48), (48, 2, 0, 48)),
    ((0, 5, 0, 48), (48, 3, 0, 48)),
    ((0, 4, 0, 48),),
)


def forward_kernel(idx, gate_x, gw, uw, dw, *refs):
    nx, nd = len(X_PARTS), len(D_PARTS)
    x_in, d_in = refs[: 2 * nx], refs[2 * nx : 2 * nx + 2 * nd]
    (x_out, d_out, score, oa, ob, ra, rb, dgt, dut, act) = refs[2 * nx + 2 * nd :][:10]
    (xv, dv, gv, uv, wv, s1, s2, s3, sem) = refs[2 * nx + 2 * nd + 10 :]
    c, y, z = idx[0], idx[1], idx[2]
    part = xv.shape[2] // NX

    def load(parts, mine, other, dst, pos, n, rows, s):
        for pieces, m, o in zip(parts, mine, other):
            for at, rel, off, size in pieces:
                row = pl.multiple_of(lax.rem(pos + rel, n) * rows + off, 8)
                for src, h in ((m, c), (o, 1 - c)):
                    pltpu.make_async_copy(
                        src.at[pl.ds(at, size), :], dst.at[h, pl.ds(row, size), :], sem.at[s]
                    ).start()

    load(X_PARTS, x_in[:nx], x_in[nx:], xv, y, NY, 96, 0)
    for w, v, s in ((gw, gv, 2), (uw, uv, 3), (dw, wv, 4)):
        for q in range(NX):
            for h in range(NC):
                pltpu.make_async_copy(
                    w.at[:, pl.ds((q * NC + h) * part, part)],
                    v.at[h, :, pl.ds(q * part, part)],
                    sem.at[s],
                ).start()
    load(D_PARTS, d_in[:nd], d_in[nd:], dv, z, NZ, 48, 1)

    def landed(v, s):
        pltpu.make_async_copy(v, v, sem.at[s]).wait()

    def product(a, w):
        def add(h, acc):
            return acc + lax.dot_general(a[h], w[h], NT, preferred_element_type=F32)

        return lax.fori_loop(0, NC, add, jnp.zeros((a.shape[1], w.shape[1]), F32))

    landed(xv, 0)
    keep_x = pltpu.make_async_copy(xv, x_out, sem.at[5])
    keep_x.start()
    landed(gv, 2)
    pre_gate = product(xv, gv)
    landed(uv, 3)
    pre_up = product(xv, uv)
    landed(dv, 1)
    keep_d = pltpu.make_async_copy(dv, d_out, sem.at[6])
    keep_d.start()
    landed(wv, 4)
    s1[...] = product(dv, wv)
    nrow = NC * SLOTS
    for a in range(NY):
        for b in range(NZ):
            s2[pl.ds((a * NZ + b) * nrow, nrow), :] = s1[pl.ds((b * NY + a) * nrow, nrow), :]
    probe = s2[...]
    sig = jax.nn.sigmoid(pre_gate)
    swished = pre_gate * sig
    active = (swished * pre_up).astype(BF)
    score[...] = jnp.sum(active.astype(F32) * probe, axis=1, keepdims=True)
    d_active = gate_x[...] * probe
    d_gate = (d_active * pre_up * sig * (1.0 + pre_gate * (1.0 - sig))).astype(BF)
    d_up = (d_active * swished).astype(BF)

    def to_dy(v):
        s1[...] = v.astype(F32)
        for a in range(NY):
            for b in range(NZ):
                s3[pl.ds((b * NY + a) * nrow, nrow), :] = s1[pl.ds((a * NZ + b) * nrow, nrow), :]
        return s3[...]

    dg_d = to_dy(d_gate).astype(BF)
    du_d = to_dy(d_up).astype(BF)
    half, ha = xv.shape[2], oa.shape[1]
    line = NZ * nrow

    def rows(h, dst_a, dst_b):
        r = jnp.dot(d_gate, gv[h, :, pl.ds(0, ha)], preferred_element_type=F32)
        r += jnp.dot(d_up, uv[h, :, pl.ds(0, ha)], preferred_element_type=F32)
        for a in range(NY):
            at = pl.multiple_of(lax.rem(a - y + NY, NY) * line, 16)
            dst_a[pl.ds(at, line), :] = r[a * line : (a + 1) * line].astype(dst_a.dtype)
        r = jnp.dot(dg_d, gv[h, :, pl.ds(ha, half - ha)], preferred_element_type=F32)
        r += jnp.dot(du_d, uv[h, :, pl.ds(ha, half - ha)], preferred_element_type=F32)
        dst_b[...] = r.astype(dst_b.dtype)

    rows(1 - c, oa, ob)
    rows(c, ra, rb)
    dgt[...] = d_gate.astype(F32).T.astype(BF)
    dut[...] = d_up.astype(F32).T.astype(BF)
    act[...] = to_dy(active).T.astype(BF)
    keep_x.wait()
    keep_d.wait()


def forward(idx, gate_x, gw, uw, dw, parts, total, half):
    hid = gw.shape[0]
    vm = pl.BlockSpec(memory_space=pltpu.VMEM)
    hbm = pl.BlockSpec(memory_space=pl.ANY)
    ha = half * 5 // 8
    hb = half - ha
    sd = jax.ShapeDtypeStruct
    return pl.pallas_call(
        forward_kernel,
        name="forward",
        in_specs=[pl.BlockSpec(memory_space=pltpu.SMEM), vm, hbm, hbm, hbm] + [hbm] * len(parts),
        out_specs=[hbm, hbm] + [vm] * 8,
        out_shape=[
            sd((NC, total, half), BF),
            sd((NC, total, half), BF),
            sd((total, 1), F32),
            sd((total, ha), BF),
            sd((total, hb), BF),
            sd((total, ha), F32),
            sd((total, hb), F32),
            sd((hid, total), BF),
            sd((hid, total), BF),
            sd((hid, total), BF),
        ],
        scratch_shapes=[
            pltpu.VMEM((NC, total, half), BF),
            pltpu.VMEM((NC, total, half), BF),
            pltpu.VMEM((NC, hid, half), BF),
            pltpu.VMEM((NC, hid, half), BF),
            pltpu.VMEM((NC, hid, half), BF),
            pltpu.VMEM((total, hid), F32),
            pltpu.VMEM((total, hid), F32),
            pltpu.VMEM((total, hid), F32),
            pltpu.SemaphoreType.DMA((7,)),
        ],
        compiler_params=pltpu.CompilerParams(vmem_limit_bytes=56 * 2**20),
        interpret=INTERPRET,
    )(idx, gate_x, gw, uw, dw, *parts)


def grads_kernel(xb, db, gate_d, dgt, dut, act, gg, gu, gd):
    xs = xb[0]
    gg[0] = jnp.dot(dgt[...], xs, preferred_element_type=F32).astype(BF)
    gu[0] = jnp.dot(dut[...], xs, preferred_element_type=F32).astype(BF)
    weighted = (gate_d[...] * db[0].astype(F32)).astype(BF)
    gd[0] = jnp.dot(act[...], weighted, preferred_element_type=F32).astype(BF)


def grads(x_rows, dy_rows, gate_d, dgt, dut, act, blk):
    hid, total = dgt.shape
    per = x_rows.shape[2] // blk
    rows = pl.BlockSpec((1, total, blk), lambda k: (k % NC, 0, k // NC))
    small = pl.BlockSpec((hid, total), lambda k: (0, 0))
    out = pl.BlockSpec((1, hid, blk), lambda k: (0, 0, k))
    sd = jax.ShapeDtypeStruct((1, hid, NC * per * blk), BF)
    return pl.pallas_call(
        grads_kernel,
        name="weight_grads",
        grid=(NC * per,),
        in_specs=[rows, rows, pl.BlockSpec((total, 1), lambda k: (0, 0)), small, small, small],
        out_specs=[out, out, out],
        out_shape=[sd, sd, sd],
        compiler_params=pltpu.CompilerParams(vmem_limit_bytes=40 * 2**20),
        interpret=INTERPRET,
    )(x_rows, dy_rows, gate_d, dgt, dut, act)


def on_device(tokens, grad_out, gate_weight, up_weight, down_weight, gate_values, chosen, counts):
    y = lax.axis_index("y")
    z = lax.axis_index("z")
    c = lax.axis_index("c")
    x = lax.axis_index("x")
    ep = (y * NZ + z) * NC + c
    tok_rows, quarter = tokens.shape
    experts = chosen.shape[0]
    total = NY * NZ * NC * SLOTS
    part = quarter // NC
    half = NX * part
    gw, uw, dw = gate_weight[0], up_weight[0], down_weight[0]
    hid = gw.shape[0]

    onehot, px, pd = picks(tokens, grad_out, chosen, counts, ep)
    send = jnp.stack([px, pd], 0).reshape(2, experts, SLOTS, NC, part)
    send = send.transpose(3, 1, 0, 2, 4).reshape(NC * experts, 2 * SLOTS, part)
    got = lax.all_to_all(send, ("c", "x"), 0, 0, tiled=True)
    got = got.reshape(NC, NX, 2, SLOTS, part).transpose(2, 0, 3, 1, 4).reshape(2, NC * SLOTS, half)
    x_own, d_own = got[0], got[1]

    nrow = NC * SLOTS
    x_send = x_own.reshape(nrow, 2, half // 2).transpose(1, 0, 2).reshape(2 * nrow, half // 2)
    x_line = lax.all_to_all(
        jnp.broadcast_to(x_send[None], (NZ, 2 * nrow, half // 2)), "z", 0, 0, tiled=True
    )
    x_line = x_line.reshape(NZ, 2, nrow, half // 2).transpose(0, 2, 1, 3).reshape(NZ * nrow, half)
    d_near = [d_own] + [lax.ppermute(d_own, "y", shift(NY, -r)) for r in (1, 2, 3)]
    d_line = jnp.concatenate([v[None] for v in d_near], 0)
    d_line = jnp.concatenate([d_line, d_line], 0)
    d_line = lax.dynamic_slice_in_dim(d_line, lax.rem(NY - y, NY), NY, 0)
    d_line = d_line.reshape(NY * nrow, half)

    ds = [d_line]
    up, dn = d_line, d_line
    for k in range(3):
        up = lax.ppermute(up, "z", shift(NZ, 1))
        dn = lax.ppermute(dn, "z", shift(NZ, -1))
        ds.append(jnp.concatenate([up, dn], 0))
        if k == 0:
            up, dn, x_line = lax.optimization_barrier((up, dn, x_line))
    hd = NY * nrow // 2
    up = lax.ppermute(up[:hd], "z", shift(NZ, 1))
    dn = lax.ppermute(dn[hd:], "z", shift(NZ, -1))
    ds.append(jnp.concatenate([up, dn], 0))
    xp = lax.ppermute(x_line, "y", shift(NY, 1))
    xm = lax.ppermute(x_line, "y", shift(NY, -1))
    hr = NZ * nrow // 2
    xo = [lax.ppermute(xp[:hr], "y", shift(NY, 1)), lax.ppermute(xm[hr:], "y", shift(NY, -1))]
    xs = [x_line, xp, xm, jnp.concatenate(xo, 0)]
    parts = xs + [swap(v) for v in xs] + ds + [swap(v) for v in ds]

    hits = slot_table(
        lax.dynamic_index_in_dim(chosen, x, 0, keepdims=False),
        lax.dynamic_index_in_dim(counts, x, 0, keepdims=False),
        tok_rows,
        total,
    )
    gate_x = jnp.sum(jnp.where(hits, gate_values[0][None, :], 0.0), axis=1)
    gate_d = gate_x.reshape(NY, NZ, nrow).transpose(1, 0, 2).reshape(total, 1)
    idx = jnp.stack([c, y, z]).astype(jnp.int32)
    x_rows, dy_rows, score, oa, ob, ra, rb, dgt, dut, act = forward(
        idx, gate_x[:, None], gw, uw, dw, parts, total, half
    )
    ha = oa.shape[1]
    line = NZ * nrow
    ob, oa = swap(ob), swap(oa)
    rb = (rb + ob.astype(F32)).astype(BF)
    b1 = lax.all_to_all(rb.reshape(NZ, NY * nrow, half - ha), "z", 0, 0, tiled=True)
    ra = ra + oa.astype(F32)
    a1 = ra[:line]
    for r in (1, 3, 2):
        piece = ra[r * line : (r + 1) * line].astype(BF)
        a1 = a1 + lax.ppermute(piece, "y", shift(NY, r)).astype(F32)
    grad_g, grad_u, grad_d = grads(x_rows, dy_rows, gate_d, dgt, dut, act, part)
    score_sum = butterfly(score[:, 0])
    a1, b1, score_sum, grad_g = lax.optimization_barrier((a1.astype(BF), b1, score_sum, grad_g))
    a2 = lax.all_to_all(a1.reshape(NZ, nrow, ha), "z", 0, 0, tiled=True)
    b1 = jnp.sum(b1.astype(F32), 0).reshape(NY, nrow, half - ha)
    b1 = jnp.concatenate([b1, b1], 0)
    b1 = lax.dynamic_slice_in_dim(b1, y, NY, 0)
    b2 = b1[0]
    for r in (1, 3, 2):
        b2 = b2 + lax.ppermute(b1[r].astype(BF), "y", shift(NY, r)).astype(F32)
    a2 = jnp.sum(a2.astype(F32), 0)
    mine_rows = jnp.concatenate([a2, b2], 1)
    back = mine_rows.reshape(NC, SLOTS, NX, part).transpose(0, 2, 1, 3).reshape(NC * NX, SLOTS, part)
    back = lax.all_to_all(back, ("c", "x"), 0, 0, tiled=True)
    back = back.reshape(NC, experts, SLOTS, part).transpose(1, 2, 0, 3).reshape(experts * SLOTS, quarter)
    tn = (((0,), (0,)), ((), ()))
    token_grad = lax.dot_general(
        onehot.astype(F32), back, tn, precision=lax.Precision.HIGHEST, preferred_element_type=F32
    ).astype(BF)

    score_grad = jnp.sum(jnp.where(hits, score_sum[:, None], 0.0), axis=0)
    return grad_g, grad_u, grad_d, token_grad, score_grad[None]


def solution(mesh):
    torus = Mesh(mesh.devices.reshape(NY, NZ, NC, NX), ("y", "z", "c", "x"))
    ep = ("y", "z", "c")
    return jax.shard_map(
        on_device,
        mesh=torus,
        in_specs=(
            P(ep, "x"),
            P(ep, "x"),
            P("x", ep, None),
            P("x", ep, None),
            P("x", ep, None),
            P("x", None),
            P(),
            P(),
        ),
        out_specs=(
            P("x", ep, None),
            P("x", ep, None),
            P("x", ep, None),
            P(ep, "x"),
            P("x", None),
        ),
        check_vma=False,
    )
```

```python
import jax
import jax.numpy as jnp
from jax import lax
from jax.experimental import pallas as pl
from jax.experimental.pallas import tpu as pltpu
from jax.sharding import Mesh
from jax.sharding import PartitionSpec as P

SLOTS = 6
NY, NZ, NC, NX = 4, 8, 2, 4
BF, F32 = jnp.bfloat16, jnp.float32
INTERPRET = False
NT = (((1,), (1,)), ((), ()))


def shift(n, s):
    return [(i, (i + s) % n) for i in range(n)]


def swap(v):
    return lax.ppermute(v, "c", [(0, 1), (1, 0)])


def pair_sum(v, axis, n, step):
    return v + lax.ppermute(v, axis, [(i, i ^ step) for i in range(n)])


def picks(tokens, grad_out, chosen, counts, ep):
    cap = chosen.shape[1]
    tok_rows = tokens.shape[0]
    col = lax.broadcasted_iota(jnp.int32, chosen.shape, 1)
    mine = (col < counts[:, None]) & (chosen // tok_rows == ep)
    before = lax.broadcasted_iota(jnp.int32, (cap, cap), 0) < lax.broadcasted_iota(
        jnp.int32, (cap, cap), 1
    )
    rank = jnp.dot(mine.astype(BF), before.astype(BF), preferred_element_type=F32).astype(jnp.int32)
    slot = lax.broadcasted_iota(jnp.int32, (1, SLOTS, 1), 1)
    hit = mine[:, None, :] & (rank[:, None, :] == slot)
    row = jnp.sum(jnp.where(hit, (chosen - ep * tok_rows)[:, None, :] + 1, 0), axis=2) - 1
    row = row.reshape(-1)
    onehot = (row[:, None] == lax.broadcasted_iota(jnp.int32, (1, tok_rows), 1)).astype(BF)
    px = jnp.dot(onehot, tokens, preferred_element_type=F32).astype(BF)
    pd = jnp.dot(onehot, grad_out, preferred_element_type=F32).astype(BF)
    return onehot, px, pd


def slot_table(chosen_e, count_e, tok_rows, total):
    cap = chosen_e.shape[0]
    col = lax.broadcasted_iota(jnp.int32, (cap,), 0)
    live = col < count_e
    block = jnp.where(live, chosen_e // tok_rows, -1)
    same = (block[:, None] == block[None, :]) & (col[:, None] < col[None, :])
    rank = jnp.sum(same.astype(jnp.int32), axis=0)
    line = (block // NC) % NZ * NY + block // (NC * NZ)
    pos = jnp.where(live, (line * NC + block % NC) * SLOTS + rank, total)
    return pos == lax.broadcasted_iota(jnp.int32, (total, cap), 0)


LINE = NY * NC * SLOTS
RING = (0, 7, 1, 6, 2, 5, 3)


def forward_kernel(idx, gate, gw, uw, dw, *refs):
    n = len(RING) + 2
    mine, other = refs[:n], refs[n : 2 * n]
    x_out, d_out, score, acts, away, home = refs[2 * n : 2 * n + 6]
    xv, dv, gv, uv, wv, sem = refs[2 * n + 6 :]
    c, z = idx[0], idx[1]
    half = xv.shape[2]
    part = half // NX
    hid = gw.shape[0]

    def place(k, rel, first, dst, s):
        row = pl.multiple_of(lax.rem(z + rel, NZ) * LINE, 16)
        for src, h in ((mine[k], c), (other[k], 1 - c)):
            pltpu.make_async_copy(
                src.at[pl.ds(first, LINE), :], dst.at[h, pl.ds(row, LINE), :], sem.at[s]
            ).start()

    def weight(w, v, s):
        for q in range(NX):
            for h in range(NC):
                pltpu.make_async_copy(
                    w.at[:, pl.ds((q * NC + h) * part, part)],
                    v.at[h, :, pl.ds(q * part, part)],
                    sem.at[s],
                ).start()

    weight(gw, gv, 2)
    for k, rel in enumerate(RING):
        place(k, rel, 0, xv, 0)
    place(n - 2, 4, 0, xv, 0)
    weight(uw, uv, 3)
    for k, rel in enumerate(RING):
        place(k, rel, LINE, dv, 1)
    place(n - 1, 4, 0, dv, 1)
    weight(dw, wv, 4)

    def landed(v, s):
        pltpu.make_async_copy(v, v, sem.at[s]).wait()

    def product(a, w):
        def add(h, acc):
            return acc + lax.dot_general(a[h], w[h], NT, preferred_element_type=F32)

        return lax.fori_loop(0, NC, add, jnp.zeros((a.shape[1], w.shape[1]), F32))

    landed(xv, 0)
    keep_x = pltpu.make_async_copy(xv, x_out, sem.at[5])
    keep_x.start()
    landed(gv, 2)
    pre_gate = product(xv, gv)
    landed(uv, 3)
    pre_up = product(xv, uv)
    landed(dv, 1)
    keep_d = pltpu.make_async_copy(dv, d_out, sem.at[6])
    keep_d.start()
    landed(wv, 4)
    probe = product(dv, wv)
    sig = jax.nn.sigmoid(pre_gate)
    swished = pre_gate * sig
    active = (swished * pre_up).astype(BF)
    score[...] = jnp.sum(active.astype(F32) * probe, axis=1, keepdims=True)
    d_active = gate[...] * probe
    d_gate = (d_active * pre_up * sig * (1.0 + pre_gate * (1.0 - sig))).astype(BF)
    d_up = (d_active * swished).astype(BF)
    acts[0] = d_gate
    acts[1] = d_up
    acts[2] = active

    def rows(h, dst):
        for q in range(NX):
            cols = pl.ds(q * part, part)
            r = jnp.dot(d_gate, gv[h, :, cols], preferred_element_type=F32)
            r += jnp.dot(d_up, uv[h, :, cols], preferred_element_type=F32)
            r = r.astype(dst.dtype)
            for a in range(NZ):
                rel = lax.rem(a - z + NZ, NZ)
                at = jnp.where(rel < 4, 7 - 2 * rel, 2 * (rel - 4)) * LINE
                dst[pl.ds(pl.multiple_of(at, 16), LINE), cols] = r[a * LINE : (a + 1) * LINE]

    rows(1 - c, away)
    rows(c, home)
    keep_x.wait()
    keep_d.wait()


def forward(idx, gate, gw, uw, dw, parts, total, half):
    hid = gw.shape[0]
    vm = pl.BlockSpec(memory_space=pltpu.VMEM)
    hbm = pl.BlockSpec(memory_space=pl.ANY)
    sd = jax.ShapeDtypeStruct
    return pl.pallas_call(
        forward_kernel,
        name="forward",
        in_specs=[pl.BlockSpec(memory_space=pltpu.SMEM), vm, hbm, hbm, hbm] + [hbm] * len(parts),
        out_specs=[hbm, hbm] + [vm] * 4,
        out_shape=[
            sd((NC, total, half), BF),
            sd((NC, total, half), BF),
            sd((total, 1), F32),
            sd((3, total, hid), BF),
            sd((total, half), BF),
            sd((total, half), F32),
        ],
        scratch_shapes=[
            pltpu.VMEM((NC, total, half), BF),
            pltpu.VMEM((NC, total, half), BF),
            pltpu.VMEM((NC, hid, half), BF),
            pltpu.VMEM((NC, hid, half), BF),
            pltpu.VMEM((NC, hid, half), BF),
            pltpu.SemaphoreType.DMA((7,)),
        ],
        compiler_params=pltpu.CompilerParams(vmem_limit_bytes=56 * 2**20),
        interpret=INTERPRET,
    )(idx, gate, gw, uw, dw, *parts)


def grads_kernel(x_rows, d_rows, gate, acts, gg, gu, gd, xv, dv, gate_v, av, tv, ov, sem, sem_x, sem_d, sem_o):
    n, total, blk = xv.shape
    small = (
        pltpu.make_async_copy(acts, av, sem.at[0]),
        pltpu.make_async_copy(gate, gate_v, sem.at[1]),
    )
    for v in small:
        v.start()

    def pair(k):
        cols = pl.ds(pl.multiple_of(k // NC * blk, blk), blk)
        h = lax.rem(k, NC)
        return (
            pltpu.make_async_copy(x_rows.at[h, :, cols], xv.at[k], sem_x.at[k]),
            pltpu.make_async_copy(d_rows.at[h, :, cols], dv.at[k], sem_d.at[k]),
        )

    @pl.loop(0, n)
    def _(k):
        for v in pair(k):
            v.start()

    for v in small:
        v.wait()
    for t in range(3):
        tv[t] = av[t].astype(F32).T.astype(BF)

    @pl.loop(0, n)
    def _(k):
        cols = pl.ds(pl.multiple_of(k * blk, blk), blk)
        for v in pair(k):
            v.wait()
        xs = xv[k]
        weighted = (gate_v[...] * dv[k].astype(F32)).astype(BF)
        for t, (rhs, dst) in enumerate(((xs, gg), (xs, gu), (weighted, gd))):
            ov[t, :, cols] = jnp.dot(tv[t], rhs, preferred_element_type=F32).astype(BF)
            pltpu.make_async_copy(ov.at[t, :, cols], dst.at[0, :, cols], sem_o.at[t]).start()

    for t, dst in enumerate((gg, gu, gd)):
        pltpu.make_async_copy(ov.at[t], dst.at[0], sem_o.at[t]).wait()


def grads(x_rows, d_rows, gate, acts, blk):
    _, total, hid = acts.shape
    width = NC * x_rows.shape[2]
    n = width // blk
    hbm = pl.BlockSpec(memory_space=pl.ANY)
    sd = jax.ShapeDtypeStruct((1, hid, width), BF)
    return pl.pallas_call(
        grads_kernel,
        name="weight_grads",
        in_specs=[hbm] * 4,
        out_specs=[hbm] * 3,
        out_shape=[sd, sd, sd],
        scratch_shapes=[
            pltpu.VMEM((n, total, blk), BF),
            pltpu.VMEM((n, total, blk), BF),
            pltpu.VMEM((total, 1), F32),
            pltpu.VMEM((3, total, hid), BF),
            pltpu.VMEM((3, hid, total), BF),
            pltpu.VMEM((3, hid, width), BF),
            pltpu.SemaphoreType.DMA((2,)),
            pltpu.SemaphoreType.DMA((n,)),
            pltpu.SemaphoreType.DMA((n,)),
            pltpu.SemaphoreType.DMA((3,)),
        ],
        compiler_params=pltpu.CompilerParams(vmem_limit_bytes=40 * 2**20),
        interpret=INTERPRET,
    )(x_rows, d_rows, gate, acts)


def on_device(tokens, grad_out, gate_weight, up_weight, down_weight, gate_values, chosen, counts):
    y = lax.axis_index("y")
    z = lax.axis_index("z")
    c = lax.axis_index("c")
    x = lax.axis_index("x")
    ep = (y * NZ + z) * NC + c
    tok_rows, quarter = tokens.shape
    experts = chosen.shape[0]
    total = NZ * LINE
    part = quarter // NC
    half = NX * part
    plane = ("y", "c", "x")

    onehot, px, pd = picks(tokens, grad_out, chosen, counts, ep)
    send = jnp.stack([px, pd], 0).reshape(2, experts, SLOTS, NC, part)
    send = send.transpose(3, 1, 0, 2, 4).reshape(1, NC * experts, 2 * SLOTS, part)
    send = jnp.broadcast_to(send, (NY,) + send.shape[1:]).reshape(-1, 2 * SLOTS, part)
    got = lax.all_to_all(send, plane, 0, 0, tiled=True)
    got = got.reshape(NY, NC, NX, 2, SLOTS, part).transpose(3, 0, 1, 4, 2, 5)
    line = got.reshape(2 * LINE, half)

    pieces = [line]
    up, dn = line, line
    for _ in range(3):
        up = lax.ppermute(up, "z", shift(NZ, 1))
        dn = lax.ppermute(dn, "z", shift(NZ, -1))
        pieces += [up, dn]
    pieces.append(lax.ppermute(up[:LINE], "z", shift(NZ, 1)))
    pieces.append(lax.ppermute(dn[LINE:], "z", shift(NZ, -1)))
    parts = pieces + [swap(v) for v in pieces]

    hits = slot_table(
        lax.dynamic_index_in_dim(chosen, x, 0, keepdims=False),
        lax.dynamic_index_in_dim(counts, x, 0, keepdims=False),
        tok_rows,
        total,
    )
    gate = jnp.sum(jnp.where(hits, gate_values[0][None, :], 0.0), axis=1)[:, None]
    idx = jnp.stack([c, z]).astype(jnp.int32)
    x_rows, d_rows, score, acts, away, home = forward(
        idx, gate, gate_weight[0], up_weight[0], down_weight[0], parts, total, half
    )

    far = swap(away[: 3 * LINE]).astype(F32) + home[: 3 * LINE]
    near = swap(away[3 * LINE :]).astype(F32) + home[3 * LINE :]
    sums = jnp.split(far, 3, 0) + jnp.split(near, 5, 0)
    hl = LINE // 2
    up = lax.ppermute(sums[0][:hl].astype(BF), "z", shift(NZ, 1))
    dn = lax.ppermute(sums[0][hl:].astype(BF), "z", shift(NZ, -1))
    up = jnp.concatenate([sums[1][:hl] + up.astype(F32), sums[1][hl:]], 0)
    dn = jnp.concatenate([sums[2][:hl], sums[2][hl:] + dn.astype(F32)], 0)
    total_score = pair_sum(score[:, 0], "c", NC, 1)
    up, dn, total_score = lax.optimization_barrier((up.astype(BF), dn.astype(BF), total_score))
    for k in (3, 5):
        up = lax.ppermute(up, "z", shift(NZ, 1)).astype(F32) + sums[k]
        dn = lax.ppermute(dn, "z", shift(NZ, -1)).astype(F32) + sums[k + 1]
        total_score = pair_sum(total_score, "y", NY, k // 2)
        up, dn, total_score = lax.optimization_barrier((up.astype(BF), dn.astype(BF), total_score))
    total_score = pair_sum(total_score, "z", NZ, 1)
    up = lax.ppermute(up.astype(BF), "z", shift(NZ, 1)).astype(F32)
    dn = lax.ppermute(dn.astype(BF), "z", shift(NZ, -1)).astype(F32)
    rows = (sums[7] + up + dn).astype(BF)

    grad_g, grad_u, grad_d = grads(x_rows, d_rows, gate, acts, part)
    rows, grad_g, grad_u, grad_d, total_score = lax.optimization_barrier(
        (rows, grad_g, grad_u, grad_d, total_score)
    )
    score_sum = pair_sum(pair_sum(total_score, "z", NZ, 2), "z", NZ, 4)
    back = rows.reshape(NY, NC, SLOTS, NX, part).transpose(0, 1, 3, 2, 4)
    back = lax.all_to_all(back.reshape(-1, SLOTS, part), plane, 0, 0, tiled=True)
    back = jnp.sum(back.reshape(NY, NC, experts, SLOTS, part).astype(F32), 0)
    back = back.transpose(1, 2, 0, 3).reshape(experts * SLOTS, quarter)
    tn = (((0,), (0,)), ((), ()))
    token_grad = lax.dot_general(
        onehot.astype(F32), back, tn, precision=lax.Precision.HIGHEST, preferred_element_type=F32
    ).astype(BF)
    score_grad = jnp.sum(jnp.where(hits, score_sum[:, None], 0.0), axis=0)
    return grad_g, grad_u, grad_d, token_grad, score_grad[None]


def solution(mesh):
    torus = Mesh(mesh.devices.reshape(NY, NZ, NC, NX), ("y", "z", "c", "x"))
    ep = ("y", "z", "c")
    return jax.shard_map(
        on_device,
        mesh=torus,
        in_specs=(
            P(ep, "x"),
            P(ep, "x"),
            P("x", ep, None),
            P("x", ep, None),
            P("x", ep, None),
            P("x", None),
            P(),
            P(),
        ),
        out_specs=(
            P("x", ep, None),
            P("x", ep, None),
            P("x", ep, None),
            P(ep, "x"),
            P("x", None),
        ),
        check_vma=False,
    )
```

```python
import functools

import jax
import jax.numpy as jnp
from jax import lax
from jax.experimental import pallas as pl
from jax.experimental.pallas import tpu as pltpu
from jax.sharding import Mesh
from jax.sharding import PartitionSpec as P

SLOTS = 6
NY, NZ, NC, NX = 4, 8, 2, 4
BF, F32 = jnp.bfloat16, jnp.float32
INTERPRET = False
NT = (((1,), (1,)), ((), ()))


def shift(n, s):
    return [(i, (i + s) % n) for i in range(n)]


def swap(v):
    return lax.ppermute(v, "c", [(0, 1), (1, 0)])


def pair_sum(v, axis, n, step):
    return v + lax.ppermute(v, axis, [(i, i ^ step) for i in range(n)])


def picks(tokens, grad_out, chosen, counts, ep):
    cap = chosen.shape[1]
    tok_rows = tokens.shape[0]
    col = lax.broadcasted_iota(jnp.int32, chosen.shape, 1)
    mine = (col < counts[:, None]) & (chosen // tok_rows == ep)
    before = lax.broadcasted_iota(jnp.int32, (cap, cap), 0) < lax.broadcasted_iota(
        jnp.int32, (cap, cap), 1
    )
    rank = jnp.dot(mine.astype(BF), before.astype(BF), preferred_element_type=F32).astype(jnp.int32)
    slot = lax.broadcasted_iota(jnp.int32, (1, SLOTS, 1), 1)
    hit = mine[:, None, :] & (rank[:, None, :] == slot)
    row = jnp.sum(jnp.where(hit, (chosen - ep * tok_rows)[:, None, :] + 1, 0), axis=2) - 1
    row = row.reshape(-1)
    onehot = (row[:, None] == lax.broadcasted_iota(jnp.int32, (1, tok_rows), 1)).astype(BF)
    px = jnp.dot(onehot, tokens, preferred_element_type=F32).astype(BF)
    pd = jnp.dot(onehot, grad_out, preferred_element_type=F32).astype(BF)
    return onehot, px, pd


def slot_table(chosen_e, count_e, tok_rows, total, z):
    cap = chosen_e.shape[0]
    col = lax.broadcasted_iota(jnp.int32, (cap,), 0)
    live = col < count_e
    block = jnp.where(live, chosen_e // tok_rows, -1)
    same = (block[:, None] == block[None, :]) & (col[:, None] < col[None, :])
    rank = jnp.sum(same.astype(jnp.int32), axis=0)
    rel = (block // NC - z) % NZ
    line = jnp.where(rel < 3, 4 - 2 * rel, jnp.where(rel > 5, 2 * rel - 11, 7))
    line = jnp.where(rel == 4, 5, jnp.where(rel == 3, 6, line))
    pos = ((line * NY + block // (NC * NZ)) * NC + block % NC) * SLOTS + rank
    pos = jnp.where(live, pos, total)
    return pos == lax.broadcasted_iota(jnp.int32, (total, cap), 0)


LINE = NY * NC * SLOTS
N_NEAR, N_FAR = 5, 3


def forward_kernel(x_src, d_src, idx, gate, gw, uw, dw, *refs):
    n = (len(refs) - 12) // 2
    mine, other = refs[:n], refs[n : 2 * n]
    x_out, d_out, score, acts, away, home = refs[2 * n : 2 * n + 6]
    xv, dv, gv, uv, wv, sem = refs[2 * n + 6 :]
    c = idx[0]
    half = xv.shape[2]
    part = half // NX

    def place(sources, dst, s):
        for i, (k, first) in enumerate(sources):
            for src, h in ((mine[k], c), (other[k], 1 - c)):
                pltpu.make_async_copy(
                    src.at[pl.ds(first, LINE), :], dst.at[h, pl.ds(i * LINE, LINE), :], sem.at[s]
                ).start()

    def weight(w, v, s):
        for q in range(NX):
            for h in range(NC):
                pltpu.make_async_copy(
                    w.at[:, pl.ds((q * NC + h) * part, part)],
                    v.at[h, :, pl.ds(q * part, part)],
                    sem.at[s],
                ).start()

    place(x_src, xv, 0)
    weight(gw, gv, 2)
    weight(uw, uv, 3)
    place(d_src, dv, 1)
    weight(dw, wv, 4)

    def landed(v, s):
        pltpu.make_async_copy(v, v, sem.at[s]).wait()

    def product(a, w):
        def add(h, acc):
            return acc + lax.dot_general(a[h], w[h], NT, preferred_element_type=F32)

        return lax.fori_loop(0, NC, add, jnp.zeros((a.shape[1], w.shape[1]), F32))

    landed(xv, 0)
    keep_x = pltpu.make_async_copy(xv, x_out, sem.at[5])
    keep_x.start()
    landed(gv, 2)
    pre_gate = product(xv, gv)
    landed(uv, 3)
    pre_up = product(xv, uv)
    landed(dv, 1)
    keep_d = pltpu.make_async_copy(dv, d_out, sem.at[6])
    keep_d.start()
    landed(wv, 4)
    probe = product(dv, wv)
    sig = jax.nn.sigmoid(pre_gate)
    swished = pre_gate * sig
    active = (swished * pre_up).astype(BF)
    score[...] = jnp.sum(active.astype(F32) * probe, axis=1, keepdims=True)
    d_active = gate[...] * probe
    d_gate = (d_active * pre_up * sig * (1.0 + pre_gate * (1.0 - sig))).astype(BF)
    d_up = (d_active * swished).astype(BF)
    acts[0] = d_gate
    acts[1] = d_up
    acts[2] = active

    for h, dst in ((1 - c, away), (c, home)):
        for q in range(NX):
            cols = pl.ds(q * part, part)
            r = jnp.dot(d_gate, gv[h, :, cols], preferred_element_type=F32)
            r += jnp.dot(d_up, uv[h, :, cols], preferred_element_type=F32)
            dst[:, cols] = r.astype(dst.dtype)
    keep_x.wait()
    keep_d.wait()


def forward(name, x_src, d_src, idx, gate, gw, uw, dw, pieces, swapped):
    hid = gw.shape[0]
    rows = gate.shape[0]
    half = pieces[0].shape[1]
    vm = pl.BlockSpec(memory_space=pltpu.VMEM)
    hbm = pl.BlockSpec(memory_space=pl.ANY)
    sd = jax.ShapeDtypeStruct
    return pl.pallas_call(
        functools.partial(forward_kernel, x_src, d_src),
        name=name,
        in_specs=[pl.BlockSpec(memory_space=pltpu.SMEM), vm] + [hbm] * (3 + 2 * len(pieces)),
        out_specs=[hbm, hbm] + [vm] * 4,
        out_shape=[
            sd((NC, rows, half), BF),
            sd((NC, rows, half), BF),
            sd((rows, 1), F32),
            sd((3, rows, hid), BF),
            sd((rows, half), BF),
            sd((rows, half), F32),
        ],
        scratch_shapes=[
            pltpu.VMEM((NC, rows, half), BF),
            pltpu.VMEM((NC, rows, half), BF),
            pltpu.VMEM((NC, hid, half), BF),
            pltpu.VMEM((NC, hid, half), BF),
            pltpu.VMEM((NC, hid, half), BF),
            pltpu.SemaphoreType.DMA((7,)),
        ],
        compiler_params=pltpu.CompilerParams(vmem_limit_bytes=48 * 2**20),
        interpret=INTERPRET,
    )(idx, gate, gw, uw, dw, *pieces, *swapped)


def grads_kernel(xn, xf, dn, df, gate, an, af, gg, gu, gd, xv, dv, gate_v, av, tv, ov, sem, sem_k, sem_o):
    n, total, blk = xv.shape
    near, far = pl.ds(0, xn.shape[1]), pl.ds(xn.shape[1], xf.shape[1])
    small = (
        pltpu.make_async_copy(an, av.at[:, near, :], sem.at[0]),
        pltpu.make_async_copy(af, av.at[:, far, :], sem.at[1]),
        pltpu.make_async_copy(gate, gate_v, sem.at[2]),
    )
    for v in small:
        v.start()

    def block(k):
        cols = pl.ds(pl.multiple_of(k // NC * blk, blk), blk)
        h = lax.rem(k, NC)
        return [
            pltpu.make_async_copy(src.at[h, :, cols], dst.at[k, at, :], sem_k.at[i, k])
            for i, (src, dst, at) in enumerate(
                ((xn, xv, near), (xf, xv, far), (dn, dv, near), (df, dv, far))
            )
        ]

    @pl.loop(0, n)
    def _(k):
        for v in block(k):
            v.start()

    for v in small:
        v.wait()
    for t in range(3):
        tv[t] = av[t].astype(F32).T.astype(BF)

    @pl.loop(0, n)
    def _(k):
        cols = pl.ds(pl.multiple_of(k * blk, blk), blk)
        for v in block(k):
            v.wait()
        xs = xv[k]
        weighted = (gate_v[...] * dv[k].astype(F32)).astype(BF)
        for t, (rhs, dst) in enumerate(((xs, gg), (xs, gu), (weighted, gd))):
            ov[t, :, cols] = jnp.dot(tv[t], rhs, preferred_element_type=F32).astype(BF)
            pltpu.make_async_copy(ov.at[t, :, cols], dst.at[0, :, cols], sem_o.at[t]).start()

    for t, dst in enumerate((gg, gu, gd)):
        pltpu.make_async_copy(ov.at[t], dst.at[0], sem_o.at[t]).wait()


def grads(xn, xf, dn, df, gate, an, af, blk):
    total, hid = gate.shape[0], an.shape[2]
    width = NC * xn.shape[2]
    n = width // blk
    hbm = pl.BlockSpec(memory_space=pl.ANY)
    sd = jax.ShapeDtypeStruct((1, hid, width), BF)
    return pl.pallas_call(
        grads_kernel,
        name="weight_grads",
        in_specs=[hbm] * 7,
        out_specs=[hbm] * 3,
        out_shape=[sd, sd, sd],
        scratch_shapes=[
            pltpu.VMEM((n, total, blk), BF),
            pltpu.VMEM((n, total, blk), BF),
            pltpu.VMEM((total, 1), F32),
            pltpu.VMEM((3, total, hid), BF),
            pltpu.VMEM((3, hid, total), BF),
            pltpu.VMEM((3, hid, width), BF),
            pltpu.SemaphoreType.DMA((3,)),
            pltpu.SemaphoreType.DMA((4, n)),
            pltpu.SemaphoreType.DMA((3,)),
        ],
        compiler_params=pltpu.CompilerParams(vmem_limit_bytes=40 * 2**20),
        interpret=INTERPRET,
    )(xn, xf, dn, df, gate, an, af)


def on_device(tokens, grad_out, gate_weight, up_weight, down_weight, gate_values, chosen, counts):
    y = lax.axis_index("y")
    z = lax.axis_index("z")
    c = lax.axis_index("c")
    x = lax.axis_index("x")
    ep = (y * NZ + z) * NC + c
    tok_rows, quarter = tokens.shape
    experts = chosen.shape[0]
    total = NZ * LINE
    part = quarter // NC
    half = NX * part
    plane = ("y", "c", "x")

    gw, uw, dw = gate_weight[0], up_weight[0], down_weight[0]

    onehot, px, pd = picks(tokens, grad_out, chosen, counts, ep)
    cut = part // 2
    send = jnp.stack([px, pd], 0).reshape(2, experts, SLOTS, NC, 2, cut)
    send = send.transpose(3, 1, 4, 0, 2, 5).reshape(1, NC * experts, 4 * SLOTS, cut)
    send = jnp.broadcast_to(send, (NY,) + send.shape[1:]).reshape(-1, 4 * SLOTS, cut)
    got = lax.all_to_all(send, plane, 0, 0, tiled=True)
    got = got.reshape(NY, NC, NX, 2, 2, SLOTS, cut).transpose(4, 0, 1, 5, 2, 3, 6)
    line = got.reshape(2 * LINE, half)

    hits = slot_table(
        lax.dynamic_index_in_dim(chosen, x, 0, keepdims=False),
        lax.dynamic_index_in_dim(counts, x, 0, keepdims=False),
        tok_rows,
        total,
        z,
    )
    gate = jnp.sum(jnp.where(hits, gate_values[0][None, :], 0.0), axis=1)[:, None]
    idx = c.astype(jnp.int32)[None]

    cut_row = N_NEAR * LINE
    pieces = [line]
    up, dn = line, line
    for _ in range(2):
        up = lax.ppermute(up, "z", shift(NZ, 1))
        dn = lax.ppermute(dn, "z", shift(NZ, -1))
        pieces += [up, dn]
    up = lax.ppermute(up, "z", shift(NZ, 1))
    dn = lax.ppermute(dn, "z", shift(NZ, -1))
    near = [(k, 0) for k in (4, 3, 2, 1, 0)]
    xn, dyn, score_n, acts_n, away, home_n = forward(
        "forward_near", near, [(k, LINE) for k, _ in near], idx, gate[:cut_row],
        gw, uw, dw, pieces, [swap(v) for v in pieces],
    )
    up, dn, away = lax.optimization_barrier((up, dn, away))
    last_x = lax.ppermute(up[:LINE], "z", shift(NZ, 1))
    last_d = lax.ppermute(dn[LINE:], "z", shift(NZ, -1))
    near_sum = swap(away).astype(F32) + home_n
    part_score = jnp.sum(jnp.where(hits[:cut_row], score_n, 0.0), axis=0)
    last_x, last_d, near_sum, part_score = lax.optimization_barrier(
        (last_x, last_d, near_sum, part_score)
    )
    pieces = [up, dn, last_x, last_d]
    xf, dyf, score_f, acts_f, away, home_f = forward(
        "forward_far", [(2, 0), (1, 0), (0, 0)], [(3, 0), (1, LINE), (0, LINE)], idx,
        gate[cut_row:], gw, uw, dw, pieces, [swap(v) for v in pieces],
    )

    sums = jnp.split(swap(away).astype(F32) + home_f, N_FAR, 0) + jnp.split(near_sum, N_NEAR, 0)
    hl = LINE // 2
    up = lax.ppermute(sums[0][:hl].astype(BF), "z", shift(NZ, 1))
    dn = lax.ppermute(sums[0][hl:].astype(BF), "z", shift(NZ, -1))
    up = sums[1] + jnp.pad(up.astype(F32), ((0, hl), (0, 0)))
    dn = sums[2] + jnp.pad(dn.astype(F32), ((hl, 0), (0, 0)))
    score = part_score + jnp.sum(jnp.where(hits[cut_row:], score_f, 0.0), axis=0)
    score = pair_sum(score, "c", NC, 1)
    up, dn, score = lax.optimization_barrier((up.astype(BF), dn.astype(BF), score))
    for k, stages in ((3, (("y", NY, 1), ("y", NY, 2))), (5, (("z", NZ, 1),))):
        up = lax.ppermute(up, "z", shift(NZ, 1)).astype(F32) + sums[k]
        dn = lax.ppermute(dn, "z", shift(NZ, -1)).astype(F32) + sums[k + 1]
        for stage in stages:
            score = pair_sum(score, *stage)
        up, dn, score = lax.optimization_barrier((up.astype(BF), dn.astype(BF), score))
    score = pair_sum(score, "z", NZ, 2)
    up = lax.ppermute(up, "z", shift(NZ, 1)).astype(F32)
    dn = lax.ppermute(dn, "z", shift(NZ, -1)).astype(F32)
    rows = (sums[7] + up + dn).astype(BF)
    grad_g, grad_u, grad_d = grads(xn, xf, dyn, dyf, gate, acts_n, acts_f, part)
    rows, grad_g, grad_u, grad_d, score = lax.optimization_barrier(
        (rows, grad_g, grad_u, grad_d, score)
    )
    score = pair_sum(score, "z", NZ, 4)

    cut = part // 4
    back = rows.reshape(NY, NC, SLOTS, NX, 4, cut).transpose(0, 1, 3, 4, 2, 5)
    back = lax.all_to_all(back.reshape(-1, 4 * SLOTS, cut), plane, 0, 0, tiled=True)
    back = jnp.sum(back.reshape(NY, NC, experts, 4, SLOTS, cut).astype(F32), 0)
    back = back.transpose(1, 3, 0, 2, 4).reshape(experts * SLOTS, quarter)
    tn = (((0,), (0,)), ((), ()))
    token_grad = lax.dot_general(
        onehot.astype(F32), back, tn, precision=lax.Precision.HIGHEST, preferred_element_type=F32
    ).astype(BF)
    return grad_g, grad_u, grad_d, token_grad, score[None]


def solution(mesh):
    torus = Mesh(mesh.devices.reshape(NY, NZ, NC, NX), ("y", "z", "c", "x"))
    ep = ("y", "z", "c")
    return jax.shard_map(
        on_device,
        mesh=torus,
        in_specs=(
            P(ep, "x"),
            P(ep, "x"),
            P("x", ep, None),
            P("x", ep, None),
            P("x", ep, None),
            P("x", None),
            P(),
            P(),
        ),
        out_specs=(
            P("x", ep, None),
            P("x", ep, None),
            P("x", ep, None),
            P(ep, "x"),
            P("x", None),
        ),
        check_vma=False,
    )
```

```python
import functools

import jax
import jax.numpy as jnp
from jax import lax
from jax.experimental import pallas as pl
from jax.experimental.pallas import tpu as pltpu
from jax.sharding import Mesh
from jax.sharding import PartitionSpec as P

SLOTS = 6
NY, NZ, NC, NX = 4, 8, 2, 4
BF, F32 = jnp.bfloat16, jnp.float32
INTERPRET = False
NT = (((1,), (1,)), ((), ()))


def shift(n, s):
    return [(i, (i + s) % n) for i in range(n)]


def swap(v):
    return lax.ppermute(v, "c", [(0, 1), (1, 0)])


def pair_sum(v, axis, n, step):
    return v + lax.ppermute(v, axis, [(i, i ^ step) for i in range(n)])


def picks(tokens, grad_out, chosen, counts, ep):
    cap = chosen.shape[1]
    tok_rows = tokens.shape[0]
    col = lax.broadcasted_iota(jnp.int32, chosen.shape, 1)
    mine = (col < counts[:, None]) & (chosen // tok_rows == ep)
    before = lax.broadcasted_iota(jnp.int32, (cap, cap), 0) < lax.broadcasted_iota(
        jnp.int32, (cap, cap), 1
    )
    rank = jnp.dot(mine.astype(BF), before.astype(BF), preferred_element_type=F32).astype(jnp.int32)
    slot = lax.broadcasted_iota(jnp.int32, (1, SLOTS, 1), 1)
    hit = mine[:, None, :] & (rank[:, None, :] == slot)
    row = jnp.sum(jnp.where(hit, (chosen - ep * tok_rows)[:, None, :] + 1, 0), axis=2) - 1
    row = row.reshape(-1)
    onehot = (row[:, None] == lax.broadcasted_iota(jnp.int32, (1, tok_rows), 1)).astype(BF)
    px = jnp.dot(onehot, tokens, preferred_element_type=F32).astype(BF)
    pd = jnp.dot(onehot, grad_out, preferred_element_type=F32).astype(BF)
    return onehot, px, pd


def slot_table(chosen_e, count_e, tok_rows, total, z):
    cap = chosen_e.shape[0]
    col = lax.broadcasted_iota(jnp.int32, (cap,), 0)
    live = col < count_e
    block = jnp.where(live, chosen_e // tok_rows, -1)
    same = (block[:, None] == block[None, :]) & (col[:, None] < col[None, :])
    rank = jnp.sum(same.astype(jnp.int32), axis=0)
    rel = (block // NC - z) % NZ
    line = jnp.where(rel < 3, 4 - 2 * rel, jnp.where(rel > 5, 2 * rel - 11, 7))
    line = jnp.where(rel == 4, 5, jnp.where(rel == 3, 6, line))
    pos = ((line * NY + block // (NC * NZ)) * NC + block % NC) * SLOTS + rank
    pos = jnp.where(live, pos, total)
    return pos == lax.broadcasted_iota(jnp.int32, (total, cap), 0)


LINE = NY * NC * SLOTS
N_NEAR, N_FAR = 5, 3


def forward_kernel(x_src, d_src, idx, gate, gw, uw, dw, *refs):
    n = (len(refs) - 12) // 2
    mine, other = refs[:n], refs[n : 2 * n]
    x_out, d_out, score, acts, away, home = refs[2 * n : 2 * n + 6]
    xv, dv, gv, uv, wv, sem = refs[2 * n + 6 :]
    c = idx[0]
    half = xv.shape[2]
    part = half // NX

    def place(sources, dst, s):
        for i, (k, first) in enumerate(sources):
            for src, h in ((mine[k], c), (other[k], 1 - c)):
                pltpu.make_async_copy(
                    src.at[pl.ds(first, LINE), :], dst.at[h, pl.ds(i * LINE, LINE), :], sem.at[s]
                ).start()

    def weight(w, v, s):
        for q in range(NX):
            for h in range(NC):
                pltpu.make_async_copy(
                    w.at[:, pl.ds((q * NC + h) * part, part)],
                    v.at[h, :, pl.ds(q * part, part)],
                    sem.at[s],
                ).start()

    place(x_src, xv, 0)
    weight(gw, gv, 2)
    weight(uw, uv, 3)
    place(d_src, dv, 1)
    weight(dw, wv, 4)

    def landed(v, s):
        pltpu.make_async_copy(v, v, sem.at[s]).wait()

    def product(a, w):
        def add(h, acc):
            return acc + lax.dot_general(a[h], w[h], NT, preferred_element_type=F32)

        return lax.fori_loop(0, NC, add, jnp.zeros((a.shape[1], w.shape[1]), F32))

    landed(xv, 0)
    keep_x = pltpu.make_async_copy(xv, x_out, sem.at[5])
    keep_x.start()
    landed(gv, 2)
    pre_gate = product(xv, gv)
    landed(uv, 3)
    pre_up = product(xv, uv)
    landed(dv, 1)
    keep_d = pltpu.make_async_copy(dv, d_out, sem.at[6])
    keep_d.start()
    landed(wv, 4)
    probe = product(dv, wv)
    sig = jax.nn.sigmoid(pre_gate)
    swished = pre_gate * sig
    active = (swished * pre_up).astype(BF)
    score[...] = jnp.sum(active.astype(F32) * probe, axis=1, keepdims=True)
    d_active = gate[...] * probe
    d_gate = (d_active * pre_up * sig * (1.0 + pre_gate * (1.0 - sig))).astype(BF)
    d_up = (d_active * swished).astype(BF)
    acts[0] = d_gate
    acts[1] = d_up
    acts[2] = active

    for h, dst in ((1 - c, away), (c, home)):
        for q in range(NX):
            cols = pl.ds(q * part, part)
            r = jnp.dot(d_gate, gv[h, :, cols], preferred_element_type=F32)
            r += jnp.dot(d_up, uv[h, :, cols], preferred_element_type=F32)
            dst[:, cols] = r.astype(dst.dtype)
    keep_x.wait()
    keep_d.wait()


def forward(name, x_src, d_src, idx, gate, gw, uw, dw, pieces, swapped):
    hid = gw.shape[0]
    rows = gate.shape[0]
    half = pieces[0].shape[1]
    vm = pl.BlockSpec(memory_space=pltpu.VMEM)
    hbm = pl.BlockSpec(memory_space=pl.ANY)
    sd = jax.ShapeDtypeStruct
    return pl.pallas_call(
        functools.partial(forward_kernel, x_src, d_src),
        name=name,
        in_specs=[pl.BlockSpec(memory_space=pltpu.SMEM), vm] + [hbm] * (3 + 2 * len(pieces)),
        out_specs=[hbm, hbm] + [vm] * 4,
        out_shape=[
            sd((NC, rows, half), BF),
            sd((NC, rows, half), BF),
            sd((rows, 1), F32),
            sd((3, rows, hid), BF),
            sd((rows, half), BF),
            sd((rows, half), F32),
        ],
        scratch_shapes=[
            pltpu.VMEM((NC, rows, half), BF),
            pltpu.VMEM((NC, rows, half), BF),
            pltpu.VMEM((NC, hid, half), BF),
            pltpu.VMEM((NC, hid, half), BF),
            pltpu.VMEM((NC, hid, half), BF),
            pltpu.SemaphoreType.DMA((7,)),
        ],
        compiler_params=pltpu.CompilerParams(vmem_limit_bytes=60 * 2**20),
        interpret=INTERPRET,
    )(idx, gate, gw, uw, dw, *pieces, *swapped)


def grads_kernel(xn, xf, dn, df, gate, an, af, gg, gu, gd, xv, dv, gate_v, av, tv, ov, sem, sem_k, sem_o):
    n, total, blk = xv.shape
    near, far = pl.ds(0, xn.shape[1]), pl.ds(xn.shape[1], xf.shape[1])
    small = (
        pltpu.make_async_copy(an, av.at[:, near, :], sem.at[0]),
        pltpu.make_async_copy(af, av.at[:, far, :], sem.at[1]),
        pltpu.make_async_copy(gate, gate_v, sem.at[2]),
    )
    for v in small:
        v.start()

    def block(k):
        cols = pl.ds(pl.multiple_of(k // NC * blk, blk), blk)
        h = lax.rem(k, NC)
        return [
            pltpu.make_async_copy(src.at[h, :, cols], dst.at[k, at, :], sem_k.at[i, k])
            for i, (src, dst, at) in enumerate(
                ((xn, xv, near), (xf, xv, far), (dn, dv, near), (df, dv, far))
            )
        ]

    @pl.loop(0, n)
    def _(k):
        for v in block(k):
            v.start()

    for v in small:
        v.wait()
    for t in range(3):
        tv[t] = av[t].astype(F32).T.astype(BF)

    @pl.loop(0, n)
    def _(k):
        cols = pl.ds(pl.multiple_of(k * blk, blk), blk)
        for v in block(k):
            v.wait()
        xs = xv[k]
        weighted = (gate_v[...] * dv[k].astype(F32)).astype(BF)
        for t, (rhs, dst) in enumerate(((xs, gg), (xs, gu), (weighted, gd))):
            ov[t, :, cols] = jnp.dot(tv[t], rhs, preferred_element_type=F32).astype(BF)
            pltpu.make_async_copy(ov.at[t, :, cols], dst.at[0, :, cols], sem_o.at[t]).start()

    for t, dst in enumerate((gg, gu, gd)):
        pltpu.make_async_copy(ov.at[t], dst.at[0], sem_o.at[t]).wait()


def grads(xn, xf, dn, df, gate, an, af, blk):
    total, hid = gate.shape[0], an.shape[2]
    width = NC * xn.shape[2]
    n = width // blk
    hbm = pl.BlockSpec(memory_space=pl.ANY)
    sd = jax.ShapeDtypeStruct((1, hid, width), BF)
    return pl.pallas_call(
        grads_kernel,
        name="weight_grads",
        in_specs=[hbm] * 7,
        out_specs=[hbm] * 3,
        out_shape=[sd, sd, sd],
        scratch_shapes=[
            pltpu.VMEM((n, total, blk), BF),
            pltpu.VMEM((n, total, blk), BF),
            pltpu.VMEM((total, 1), F32),
            pltpu.VMEM((3, total, hid), BF),
            pltpu.VMEM((3, hid, total), BF),
            pltpu.VMEM((3, hid, width), BF),
            pltpu.SemaphoreType.DMA((3,)),
            pltpu.SemaphoreType.DMA((4, n)),
            pltpu.SemaphoreType.DMA((3,)),
        ],
        compiler_params=pltpu.CompilerParams(vmem_limit_bytes=60 * 2**20),
        interpret=INTERPRET,
    )(xn, xf, dn, df, gate, an, af)


def on_device(tokens, grad_out, gate_weight, up_weight, down_weight, gate_values, chosen, counts):
    y = lax.axis_index("y")
    z = lax.axis_index("z")
    c = lax.axis_index("c")
    x = lax.axis_index("x")
    ep = (y * NZ + z) * NC + c
    tok_rows, quarter = tokens.shape
    experts = chosen.shape[0]
    total = NZ * LINE
    part = quarter // NC
    half = NX * part
    plane = ("y", "c", "x")

    gw, uw, dw = gate_weight[0], up_weight[0], down_weight[0]

    onehot, px, pd = picks(tokens, grad_out, chosen, counts, ep)
    cut = part // 2
    send = jnp.stack([px, pd], 0).reshape(2, experts, SLOTS, NC, 2, cut)
    send = send.transpose(3, 1, 4, 0, 2, 5).reshape(1, NC * experts, 4 * SLOTS, cut)
    send = jnp.broadcast_to(send, (NY,) + send.shape[1:]).reshape(-1, 4 * SLOTS, cut)
    got = lax.all_to_all(send, plane, 0, 0, tiled=True)
    got = got.reshape(NY, NC, NX, 2, 2, SLOTS, cut).transpose(4, 0, 1, 5, 2, 3, 6)
    line = got.reshape(2 * LINE, half)

    hits = slot_table(
        lax.dynamic_index_in_dim(chosen, x, 0, keepdims=False),
        lax.dynamic_index_in_dim(counts, x, 0, keepdims=False),
        tok_rows,
        total,
        z,
    )
    gate = jnp.sum(jnp.where(hits, gate_values[0][None, :], 0.0), axis=1)[:, None]
    idx = c.astype(jnp.int32)[None]

    cut_row = N_NEAR * LINE
    pieces = [line]
    up, dn = line, line
    for _ in range(2):
        up = lax.ppermute(up, "z", shift(NZ, 1))
        dn = lax.ppermute(dn, "z", shift(NZ, -1))
        pieces += [up, dn]
    up = lax.ppermute(up, "z", shift(NZ, 1))
    dn = lax.ppermute(dn, "z", shift(NZ, -1))
    near = [(k, 0) for k in (4, 3, 2, 1, 0)]
    xn, dyn, score_n, acts_n, away, home_n = forward(
        "forward_near", near, [(k, LINE) for k, _ in near], idx, gate[:cut_row],
        gw, uw, dw, pieces, [swap(v) for v in pieces],
    )
    up, dn, away = lax.optimization_barrier((up, dn, away))
    last_x = lax.ppermute(up[:LINE], "z", shift(NZ, 1))
    last_d = lax.ppermute(dn[LINE:], "z", shift(NZ, -1))
    near_sum = swap(away).astype(F32) + home_n
    part_score = jnp.sum(jnp.where(hits[:cut_row], score_n, 0.0), axis=0)
    last_x, last_d, near_sum, part_score = lax.optimization_barrier(
        (last_x, last_d, near_sum, part_score)
    )
    pieces = [up, dn, last_x, last_d]
    xf, dyf, score_f, acts_f, away, home_f = forward(
        "forward_far", [(2, 0), (1, 0), (0, 0)], [(3, 0), (1, LINE), (0, LINE)], idx,
        gate[cut_row:], gw, uw, dw, pieces, [swap(v) for v in pieces],
    )

    sums = jnp.split(swap(away).astype(F32) + home_f, N_FAR, 0) + jnp.split(near_sum, N_NEAR, 0)
    hl = LINE // 2
    up = lax.ppermute(sums[0][:hl].astype(BF), "z", shift(NZ, 1))
    dn = lax.ppermute(sums[0][hl:].astype(BF), "z", shift(NZ, -1))
    up = sums[1] + jnp.pad(up.astype(F32), ((0, hl), (0, 0)))
    dn = sums[2] + jnp.pad(dn.astype(F32), ((hl, 0), (0, 0)))
    score = part_score + jnp.sum(jnp.where(hits[cut_row:], score_f, 0.0), axis=0)
    score = pair_sum(score, "z", NZ, 4)
    up, dn, score = lax.optimization_barrier((up.astype(BF), dn.astype(BF), score))
    for k in (3, 5):
        up = lax.ppermute(up, "z", shift(NZ, 1)).astype(F32) + sums[k]
        dn = lax.ppermute(dn, "z", shift(NZ, -1)).astype(F32) + sums[k + 1]
        if k == 3:
            score = score + sum(lax.ppermute(score, "y", shift(NY, r)) for r in (1, 2, 3))
        else:
            score = pair_sum(score, "z", NZ, 2)
        up, dn, score = lax.optimization_barrier((up.astype(BF), dn.astype(BF), score))
    score = pair_sum(score, "z", NZ, 1)
    up = lax.ppermute(up, "z", shift(NZ, 1)).astype(F32)
    dn = lax.ppermute(dn, "z", shift(NZ, -1)).astype(F32)
    rows = (sums[7] + up + dn).astype(BF)
    grad_g, grad_u, grad_d = grads(xn, xf, dyn, dyf, gate, acts_n, acts_f, part)
    rows, grad_g, grad_u, grad_d, score = lax.optimization_barrier(
        (rows, grad_g, grad_u, grad_d, score)
    )
    score = pair_sum(score, "c", NC, 1)

    cut = part // 4
    back = rows.reshape(NY, NC, SLOTS, NX, 4, cut).transpose(0, 1, 3, 4, 2, 5)
    back = lax.all_to_all(back.reshape(-1, 4 * SLOTS, cut), plane, 0, 0, tiled=True)
    back = jnp.sum(back.reshape(NY, NC, experts, 4, SLOTS, cut).astype(F32), 0)
    back = back.transpose(1, 3, 0, 2, 4).reshape(experts * SLOTS, quarter)
    tn = (((0,), (0,)), ((), ()))
    token_grad = lax.dot_general(
        onehot.astype(F32), back, tn, precision=lax.Precision.HIGHEST, preferred_element_type=F32
    ).astype(BF)
    return grad_g, grad_u, grad_d, token_grad, score[None]


def solution(mesh):
    torus = Mesh(mesh.devices.reshape(NY, NZ, NC, NX), ("y", "z", "c", "x"))
    ep = ("y", "z", "c")
    return jax.shard_map(
        on_device,
        mesh=torus,
        in_specs=(
            P(ep, "x"),
            P(ep, "x"),
            P("x", ep, None),
            P("x", ep, None),
            P("x", ep, None),
            P("x", None),
            P(),
            P(),
        ),
        out_specs=(
            P("x", ep, None),
            P("x", ep, None),
            P("x", ep, None),
            P(ep, "x"),
            P("x", None),
        ),
        check_vma=False,
    )
```

```python
import functools

import jax
import jax.numpy as jnp
from jax import lax
from jax.experimental import pallas as pl
from jax.experimental.pallas import tpu as pltpu
from jax.sharding import Mesh
from jax.sharding import PartitionSpec as P

SLOTS = 6
NY, NZ, NC, NX = 4, 8, 2, 4
BF, F32 = jnp.bfloat16, jnp.float32
INTERPRET = False
NT = (((1,), (1,)), ((), ()))


def shift(n, s):
    return [(i, (i + s) % n) for i in range(n)]


def swap(v):
    return lax.ppermute(v, "c", [(0, 1), (1, 0)])


def picks(tokens, grad_out, chosen, counts, ep):
    cap = chosen.shape[1]
    tok_rows = tokens.shape[0]
    col = lax.broadcasted_iota(jnp.int32, chosen.shape, 1)
    mine = (col < counts[:, None]) & (chosen // tok_rows == ep)
    before = lax.broadcasted_iota(jnp.int32, (cap, cap), 0) < lax.broadcasted_iota(
        jnp.int32, (cap, cap), 1
    )
    rank = jnp.dot(mine.astype(BF), before.astype(BF), preferred_element_type=F32).astype(jnp.int32)
    slot = lax.broadcasted_iota(jnp.int32, (1, SLOTS, 1), 1)
    hit = mine[:, None, :] & (rank[:, None, :] == slot)
    row = jnp.sum(jnp.where(hit, (chosen - ep * tok_rows)[:, None, :] + 1, 0), axis=2) - 1
    row = row.reshape(-1)
    onehot = (row[:, None] == lax.broadcasted_iota(jnp.int32, (1, tok_rows), 1)).astype(BF)
    px = jnp.dot(onehot, tokens, preferred_element_type=F32).astype(BF)
    pd = jnp.dot(onehot, grad_out, preferred_element_type=F32).astype(BF)
    return onehot, px, pd


def slot_table(chosen_e, count_e, tok_rows, total, z):
    cap = chosen_e.shape[0]
    col = lax.broadcasted_iota(jnp.int32, (cap,), 0)
    live = col < count_e
    block = jnp.where(live, chosen_e // tok_rows, -1)
    same = (block[:, None] == block[None, :]) & (col[:, None] < col[None, :])
    rank = jnp.sum(same.astype(jnp.int32), axis=0)
    rel = (block // NC - z) % NZ
    line = jnp.where(rel < 4, 7 - 2 * rel, 2 * rel - 8)
    pos = ((line * NY + block // (NC * NZ)) * NC + block % NC) * SLOTS + rank
    pos = jnp.where(live, pos, total)
    return pos == lax.broadcasted_iota(jnp.int32, (total, cap), 0)


LINE = NY * NC * SLOTS
N_NEAR, N_FAR = 5, 3


def forward_kernel(x_src, d_src, idx, gate, gw, uw, dw, *refs):
    n = (len(refs) - 14) // 2
    mine, other = refs[:n], refs[n : 2 * n]
    x_out, d_out, score, acts, far_away, away, far_home, home = refs[2 * n : 2 * n + 8]
    xv, dv, gv, uv, wv, sem = refs[2 * n + 8 :]
    c = idx[0]
    half = xv.shape[2]
    part = half // NX

    def place(sources, dst, s):
        for i, (k, first) in enumerate(sources):
            for src, h in ((mine[k], c), (other[k], 1 - c)):
                pltpu.make_async_copy(
                    src.at[pl.ds(first, LINE), :], dst.at[h, pl.ds(i * LINE, LINE), :], sem.at[s]
                ).start()

    def weight(w, v, s):
        for q in range(NX):
            for h in range(NC):
                pltpu.make_async_copy(
                    w.at[:, pl.ds((q * NC + h) * part, part)],
                    v.at[h, :, pl.ds(q * part, part)],
                    sem.at[s],
                ).start()

    place(x_src, xv, 0)
    weight(gw, gv, 2)
    weight(uw, uv, 3)
    place(d_src, dv, 1)
    weight(dw, wv, 4)

    def landed(v, s):
        pltpu.make_async_copy(v, v, sem.at[s]).wait()

    def product(a, w):
        def add(h, acc):
            return acc + lax.dot_general(a[h], w[h], NT, preferred_element_type=F32)

        return lax.fori_loop(0, NC, add, jnp.zeros((a.shape[1], w.shape[1]), F32))

    landed(xv, 0)
    keep_x = pltpu.make_async_copy(xv, x_out, sem.at[5])
    keep_x.start()
    landed(gv, 2)
    pre_gate = product(xv, gv)
    landed(uv, 3)
    pre_up = product(xv, uv)
    landed(dv, 1)
    keep_d = pltpu.make_async_copy(dv, d_out, sem.at[6])
    keep_d.start()
    landed(wv, 4)
    probe = product(dv, wv)
    sig = jax.nn.sigmoid(pre_gate)
    swished = pre_gate * sig
    active = (swished * pre_up).astype(BF)
    score[...] = jnp.sum(active.astype(F32) * probe, axis=1, keepdims=True)
    d_active = gate[...] * probe
    d_gate = (d_active * pre_up * sig * (1.0 + pre_gate * (1.0 - sig))).astype(BF)
    d_up = (d_active * swished).astype(BF)
    acts[0] = d_gate
    acts[1] = d_up
    acts[2] = active

    cut = far_away.shape[0]
    for h, far, near in ((1 - c, far_away, away), (c, far_home, home)):
        for q in range(NX):
            cols = pl.ds(q * part, part)
            r = jnp.dot(d_gate, gv[h, :, cols], preferred_element_type=F32)
            r += jnp.dot(d_up, uv[h, :, cols], preferred_element_type=F32)
            r = r.astype(far.dtype)
            far[:, cols] = r[:cut]
            near[:, cols] = r[cut:]
    keep_x.wait()
    keep_d.wait()


def forward(x_src, d_src, idx, gate, gw, uw, dw, pieces, swapped):
    hid = gw.shape[0]
    rows = gate.shape[0]
    half = pieces[0].shape[1]
    vm = pl.BlockSpec(memory_space=pltpu.VMEM)
    hbm = pl.BlockSpec(memory_space=pl.ANY)
    sd = jax.ShapeDtypeStruct
    return pl.pallas_call(
        functools.partial(forward_kernel, x_src, d_src),
        name="forward",
        in_specs=[pl.BlockSpec(memory_space=pltpu.SMEM), vm] + [hbm] * (3 + 2 * len(pieces)),
        out_specs=[hbm, hbm] + [vm] * 6,
        out_shape=[
            sd((NC, rows, half), BF),
            sd((NC, rows, half), BF),
            sd((rows, 1), F32),
            sd((3, rows, hid), BF),
            sd((N_FAR * LINE, half), BF),
            sd((N_NEAR * LINE, half), BF),
            sd((N_FAR * LINE, half), F32),
            sd((N_NEAR * LINE, half), F32),
        ],
        scratch_shapes=[
            pltpu.VMEM((NC, rows, half), BF),
            pltpu.VMEM((NC, rows, half), BF),
            pltpu.VMEM((NC, hid, half), BF),
            pltpu.VMEM((NC, hid, half), BF),
            pltpu.VMEM((NC, hid, half), BF),
            pltpu.SemaphoreType.DMA((7,)),
        ],
        compiler_params=pltpu.CompilerParams(vmem_limit_bytes=60 * 2**20),
        interpret=INTERPRET,
    )(idx, gate, gw, uw, dw, *pieces, *swapped)


def grads_kernel(x_rows, d_rows, gate, acts, gg, gu, gd, xv, dv, gate_v, av, tv, ov, sem, sem_x, sem_d, sem_o):
    n, total, blk = xv.shape
    small = (
        pltpu.make_async_copy(acts, av, sem.at[0]),
        pltpu.make_async_copy(gate, gate_v, sem.at[1]),
    )
    for v in small:
        v.start()

    def pair(k):
        cols = pl.ds(pl.multiple_of(k // NC * blk, blk), blk)
        h = lax.rem(k, NC)
        return (
            pltpu.make_async_copy(x_rows.at[h, :, cols], xv.at[k], sem_x.at[k]),
            pltpu.make_async_copy(d_rows.at[h, :, cols], dv.at[k], sem_d.at[k]),
        )

    @pl.loop(0, n)
    def _(k):
        for v in pair(k):
            v.start()

    for v in small:
        v.wait()
    for t in range(3):
        tv[t] = av[t].astype(F32).T.astype(BF)

    @pl.loop(0, n)
    def _(k):
        cols = pl.ds(pl.multiple_of(k * blk, blk), blk)
        for v in pair(k):
            v.wait()
        xs = xv[k]
        weighted = (gate_v[...] * dv[k].astype(F32)).astype(BF)
        for t, (rhs, dst) in enumerate(((xs, gg), (xs, gu), (weighted, gd))):
            ov[t, :, cols] = jnp.dot(tv[t], rhs, preferred_element_type=F32).astype(BF)
            pltpu.make_async_copy(ov.at[t, :, cols], dst.at[0, :, cols], sem_o.at[t]).start()

    for t, dst in enumerate((gg, gu, gd)):
        pltpu.make_async_copy(ov.at[t], dst.at[0], sem_o.at[t]).wait()


def grads(x_rows, d_rows, gate, acts, blk):
    _, total, hid = acts.shape
    width = NC * x_rows.shape[2]
    n = width // blk
    hbm = pl.BlockSpec(memory_space=pl.ANY)
    sd = jax.ShapeDtypeStruct((1, hid, width), BF)
    return pl.pallas_call(
        grads_kernel,
        name="weight_grads",
        in_specs=[hbm] * 4,
        out_specs=[hbm] * 3,
        out_shape=[sd, sd, sd],
        scratch_shapes=[
            pltpu.VMEM((n, total, blk), BF),
            pltpu.VMEM((n, total, blk), BF),
            pltpu.VMEM((total, 1), F32),
            pltpu.VMEM((3, total, hid), BF),
            pltpu.VMEM((3, hid, total), BF),
            pltpu.VMEM((3, hid, width), BF),
            pltpu.SemaphoreType.DMA((2,)),
            pltpu.SemaphoreType.DMA((n,)),
            pltpu.SemaphoreType.DMA((n,)),
            pltpu.SemaphoreType.DMA((3,)),
        ],
        compiler_params=pltpu.CompilerParams(vmem_limit_bytes=60 * 2**20),
        interpret=INTERPRET,
    )(x_rows, d_rows, gate, acts)


def on_device(tokens, grad_out, gate_weight, up_weight, down_weight, gate_values, chosen, counts):
    y = lax.axis_index("y")
    z = lax.axis_index("z")
    c = lax.axis_index("c")
    x = lax.axis_index("x")
    ep = (y * NZ + z) * NC + c
    tok_rows, quarter = tokens.shape
    experts = chosen.shape[0]
    total = NZ * LINE
    part = quarter // NC
    half = NX * part
    plane = ("y", "c", "x")

    gw, uw, dw = gate_weight[0], up_weight[0], down_weight[0]

    onehot, px, pd = picks(tokens, grad_out, chosen, counts, ep)
    cut = part // 2
    send = jnp.stack([px, pd], 0).reshape(2, experts, SLOTS, NC, 2, cut)
    send = send.transpose(3, 1, 4, 0, 2, 5).reshape(1, NC * experts, 4 * SLOTS, cut)
    send = jnp.broadcast_to(send, (NY,) + send.shape[1:]).reshape(-1, 4 * SLOTS, cut)
    got = lax.all_to_all(send, plane, 0, 0, tiled=True)
    got = got.reshape(NY, NC, NX, 2, 2, SLOTS, cut).transpose(4, 0, 1, 5, 2, 3, 6)
    line = got.reshape(2 * LINE, half)

    hits = slot_table(
        lax.dynamic_index_in_dim(chosen, x, 0, keepdims=False),
        lax.dynamic_index_in_dim(counts, x, 0, keepdims=False),
        tok_rows,
        total,
        z,
    )
    gate = jnp.sum(jnp.where(hits, gate_values[0][None, :], 0.0), axis=1)[:, None]
    idx = c.astype(jnp.int32)[None]

    pieces = [line]
    up, dn = line, line
    for k in range(3):
        if k == 2:
            up, dn, gate = lax.optimization_barrier((up, dn, gate))
        up = lax.ppermute(up, "z", shift(NZ, 1))
        dn = lax.ppermute(dn, "z", shift(NZ, -1))
        pieces += [up, dn]
    pieces.append(lax.ppermute(up[:LINE], "z", shift(NZ, 1)))
    pieces.append(lax.ppermute(dn[LINE:], "z", shift(NZ, -1)))
    order = list(range(6, -1, -1))
    x_rows, d_rows, score, acts, far_away, away, far_home, home = forward(
        [(7, 0)] + [(k, 0) for k in order], [(8, 0)] + [(k, LINE) for k in order],
        idx, gate, gw, uw, dw, pieces, [swap(v) for v in pieces],
    )

    far_away, away = swap(far_away), swap(away)
    sums = jnp.split(far_away.astype(F32) + far_home, N_FAR, 0)
    sums += jnp.split(away.astype(F32) + home, N_NEAR, 0)
    score = jnp.sum(jnp.where(hits, score, 0.0), axis=0)
    up_s = dn_s = score
    hl = LINE // 2
    up, dn = sums[0][:hl].astype(BF), sums[0][hl:].astype(BF)
    for k in range(4):
        n = up.shape[0]
        up = lax.ppermute(up, "z", shift(NZ, 1)).astype(F32)
        dn = lax.ppermute(dn, "z", shift(NZ, -1)).astype(F32)
        up_s = lax.ppermute(up_s, "z", shift(NZ, 1))
        score = score + up_s
        if k < 3:
            dn_s = lax.ppermute(dn_s, "z", shift(NZ, -1))
            score = score + dn_s
            if k == 0:
                up = jnp.pad(up, ((0, LINE - n), (0, 0)))
                dn = jnp.pad(dn, ((LINE - n, 0), (0, 0)))
            up, dn = sums[2 * k + 1] + up, sums[2 * k + 2] + dn
            up, dn = up.astype(BF), dn.astype(BF)
            if k < 2:
                up, dn, up_s, dn_s = lax.optimization_barrier((up, dn, up_s, dn_s))
            else:
                up, dn, up_s, acts = lax.optimization_barrier((up, dn, up_s, acts))
    rows = (sums[7] + up + dn).astype(BF)
    grad_g, grad_u, grad_d = grads(x_rows, d_rows, gate, acts, part)
    rows, grad_g, grad_u, grad_d, score = lax.optimization_barrier(
        (rows, grad_g, grad_u, grad_d, score)
    )
    score = score + sum(lax.ppermute(score, "y", shift(NY, r)) for r in (1, 2, 3))
    score = score + swap(score)

    cut = part // 4
    back = rows.reshape(NY, NC, SLOTS, NX, 4, cut).transpose(0, 1, 3, 4, 2, 5)
    back = lax.all_to_all(back.reshape(-1, 4 * SLOTS, cut), plane, 0, 0, tiled=True)
    back = jnp.sum(back.reshape(NY, NC, experts, 4, SLOTS, cut).astype(F32), 0)
    back = back.transpose(1, 3, 0, 2, 4).reshape(experts * SLOTS, quarter)
    tn = (((0,), (0,)), ((), ()))
    token_grad = lax.dot_general(
        onehot.astype(F32), back, tn, precision=lax.Precision.HIGHEST, preferred_element_type=F32
    ).astype(BF)
    return grad_g, grad_u, grad_d, token_grad, score[None]


def solution(mesh):
    torus = Mesh(mesh.devices.reshape(NY, NZ, NC, NX), ("y", "z", "c", "x"))
    ep = ("y", "z", "c")
    return jax.shard_map(
        on_device,
        mesh=torus,
        in_specs=(
            P(ep, "x"),
            P(ep, "x"),
            P("x", ep, None),
            P("x", ep, None),
            P("x", ep, None),
            P("x", None),
            P(),
            P(),
        ),
        out_specs=(
            P("x", ep, None),
            P("x", ep, None),
            P("x", ep, None),
            P(ep, "x"),
            P("x", None),
        ),
        check_vma=False,
    )
```

```python
import functools

import jax
import jax.numpy as jnp
from jax import lax
from jax.experimental import pallas as pl
from jax.experimental.pallas import tpu as pltpu
from jax.sharding import Mesh
from jax.sharding import PartitionSpec as P

SLOTS = 6
NY, NZ, NC, NX = 4, 8, 2, 4
BF, F32 = jnp.bfloat16, jnp.float32
INTERPRET = False
NT = (((1,), (1,)), ((), ()))


def shift(n, s):
    return [(i, (i + s) % n) for i in range(n)]


def swap(v):
    return lax.ppermute(v, "c", [(0, 1), (1, 0)])


def pair_sum(v, axis, n, step):
    return v + lax.ppermute(v, axis, [(i, i ^ step) for i in range(n)])


def picks(tokens, grad_out, chosen, counts, ep):
    cap = chosen.shape[1]
    tok_rows = tokens.shape[0]
    col = lax.broadcasted_iota(jnp.int32, chosen.shape, 1)
    mine = (col < counts[:, None]) & (chosen // tok_rows == ep)
    before = lax.broadcasted_iota(jnp.int32, (cap, cap), 0) < lax.broadcasted_iota(
        jnp.int32, (cap, cap), 1
    )
    rank = jnp.dot(mine.astype(BF), before.astype(BF), preferred_element_type=F32).astype(jnp.int32)
    slot = lax.broadcasted_iota(jnp.int32, (1, SLOTS, 1), 1)
    hit = mine[:, None, :] & (rank[:, None, :] == slot)
    row = jnp.sum(jnp.where(hit, (chosen - ep * tok_rows)[:, None, :] + 1, 0), axis=2) - 1
    row = row.reshape(-1)
    onehot = (row[:, None] == lax.broadcasted_iota(jnp.int32, (1, tok_rows), 1)).astype(BF)
    px = jnp.dot(onehot, tokens, preferred_element_type=F32).astype(BF)
    pd = jnp.dot(onehot, grad_out, preferred_element_type=F32).astype(BF)
    return onehot, px, pd


def slot_table(chosen_e, count_e, tok_rows, total, z):
    cap = chosen_e.shape[0]
    col = lax.broadcasted_iota(jnp.int32, (cap,), 0)
    live = col < count_e
    block = jnp.where(live, chosen_e // tok_rows, -1)
    same = (block[:, None] == block[None, :]) & (col[:, None] < col[None, :])
    rank = jnp.sum(same.astype(jnp.int32), axis=0)
    rel = (block // NC - z) % NZ
    line = jnp.where(rel < 4, 7 - 2 * rel, 2 * rel - 8)
    pos = ((line * NY + block // (NC * NZ)) * NC + block % NC) * SLOTS + rank
    pos = jnp.where(live, pos, total)
    return pos == lax.broadcasted_iota(jnp.int32, (total, cap), 0)


LINE = NY * NC * SLOTS
N_NEAR, N_FAR = 5, 3


def forward_kernel(x_src, d_src, idx, gate, gw, uw, dw, *refs):
    n = (len(refs) - 14) // 2
    mine, other = refs[:n], refs[n : 2 * n]
    x_out, d_out, score, acts, far_away, away, far_home, home = refs[2 * n : 2 * n + 8]
    xv, dv, gv, uv, wv, sem = refs[2 * n + 8 :]
    c = idx[0]
    half = xv.shape[2]
    part = half // NX

    def place(sources, dst, s):
        for i, (k, first) in enumerate(sources):
            for src, h in ((mine[k], c), (other[k], 1 - c)):
                pltpu.make_async_copy(
                    src.at[pl.ds(first, LINE), :], dst.at[h, pl.ds(i * LINE, LINE), :], sem.at[s]
                ).start()

    def weight(w, v, s):
        for q in range(NX):
            for h in range(NC):
                pltpu.make_async_copy(
                    w.at[:, pl.ds((q * NC + h) * part, part)],
                    v.at[h, :, pl.ds(q * part, part)],
                    sem.at[s],
                ).start()

    place(x_src, xv, 0)
    weight(gw, gv, 2)
    weight(uw, uv, 3)
    place(d_src, dv, 1)
    weight(dw, wv, 4)

    def landed(v, s):
        pltpu.make_async_copy(v, v, sem.at[s]).wait()

    def product(a, w):
        def add(h, acc):
            return acc + lax.dot_general(a[h], w[h], NT, preferred_element_type=F32)

        return lax.fori_loop(0, NC, add, jnp.zeros((a.shape[1], w.shape[1]), F32))

    landed(xv, 0)
    keep_x = pltpu.make_async_copy(xv, x_out, sem.at[5])
    keep_x.start()
    landed(gv, 2)
    pre_gate = product(xv, gv)
    landed(uv, 3)
    pre_up = product(xv, uv)
    landed(dv, 1)
    keep_d = pltpu.make_async_copy(dv, d_out, sem.at[6])
    keep_d.start()
    landed(wv, 4)
    probe = product(dv, wv)
    sig = jax.nn.sigmoid(pre_gate)
    swished = pre_gate * sig
    active = (swished * pre_up).astype(BF)
    score[...] = jnp.sum(active.astype(F32) * probe, axis=1, keepdims=True)
    d_active = gate[...] * probe
    d_gate = (d_active * pre_up * sig * (1.0 + pre_gate * (1.0 - sig))).astype(BF)
    d_up = (d_active * swished).astype(BF)
    acts[0] = d_gate
    acts[1] = d_up
    acts[2] = active

    cut = far_away.shape[0]
    for h, far, near in ((1 - c, far_away, away), (c, far_home, home)):
        for q in range(NX):
            cols = pl.ds(q * part, part)
            r = jnp.dot(d_gate, gv[h, :, cols], preferred_element_type=F32)
            r += jnp.dot(d_up, uv[h, :, cols], preferred_element_type=F32)
            r = r.astype(far.dtype)
            far[:, cols] = r[:cut]
            near[:, cols] = r[cut:]
    keep_x.wait()
    keep_d.wait()


def forward(x_src, d_src, idx, gate, gw, uw, dw, pieces, swapped):
    hid = gw.shape[0]
    rows = gate.shape[0]
    half = pieces[0].shape[1]
    vm = pl.BlockSpec(memory_space=pltpu.VMEM)
    hbm = pl.BlockSpec(memory_space=pl.ANY)
    sd = jax.ShapeDtypeStruct
    return pl.pallas_call(
        functools.partial(forward_kernel, x_src, d_src),
        name="forward",
        in_specs=[pl.BlockSpec(memory_space=pltpu.SMEM), vm] + [hbm] * (3 + 2 * len(pieces)),
        out_specs=[hbm, hbm] + [vm] * 6,
        out_shape=[
            sd((NC, rows, half), BF),
            sd((NC, rows, half), BF),
            sd((rows, 1), F32),
            sd((3, rows, hid), BF),
            sd((N_FAR * LINE, half), BF),
            sd((N_NEAR * LINE, half), BF),
            sd((N_FAR * LINE, half), F32),
            sd((N_NEAR * LINE, half), F32),
        ],
        scratch_shapes=[
            pltpu.VMEM((NC, rows, half), BF),
            pltpu.VMEM((NC, rows, half), BF),
            pltpu.VMEM((NC, hid, half), BF),
            pltpu.VMEM((NC, hid, half), BF),
            pltpu.VMEM((NC, hid, half), BF),
            pltpu.SemaphoreType.DMA((7,)),
        ],
        compiler_params=pltpu.CompilerParams(vmem_limit_bytes=60 * 2**20),
        interpret=INTERPRET,
    )(idx, gate, gw, uw, dw, *pieces, *swapped)


def grads_kernel(x_rows, d_rows, gate, acts, gg, gu, gd, xv, dv, gate_v, av, tv, ov, sem, sem_x, sem_d, sem_o):
    n, total, blk = xv.shape
    small = (
        pltpu.make_async_copy(acts, av, sem.at[0]),
        pltpu.make_async_copy(gate, gate_v, sem.at[1]),
    )
    for v in small:
        v.start()

    def pair(k):
        cols = pl.ds(pl.multiple_of(k // NC * blk, blk), blk)
        h = lax.rem(k, NC)
        return (
            pltpu.make_async_copy(x_rows.at[h, :, cols], xv.at[k], sem_x.at[k]),
            pltpu.make_async_copy(d_rows.at[h, :, cols], dv.at[k], sem_d.at[k]),
        )

    @pl.loop(0, n)
    def _(k):
        for v in pair(k):
            v.start()

    for v in small:
        v.wait()
    for t in range(3):
        tv[t] = av[t].astype(F32).T.astype(BF)

    @pl.loop(0, n)
    def _(k):
        cols = pl.ds(pl.multiple_of(k * blk, blk), blk)
        for v in pair(k):
            v.wait()
        xs = xv[k]
        weighted = (gate_v[...] * dv[k].astype(F32)).astype(BF)
        for t, (rhs, dst) in enumerate(((xs, gg), (xs, gu), (weighted, gd))):
            ov[t, :, cols] = jnp.dot(tv[t], rhs, preferred_element_type=F32).astype(BF)
            pltpu.make_async_copy(ov.at[t, :, cols], dst.at[0, :, cols], sem_o.at[t]).start()

    for t, dst in enumerate((gg, gu, gd)):
        pltpu.make_async_copy(ov.at[t], dst.at[0], sem_o.at[t]).wait()


def grads(x_rows, d_rows, gate, acts, blk):
    _, total, hid = acts.shape
    width = NC * x_rows.shape[2]
    n = width // blk
    hbm = pl.BlockSpec(memory_space=pl.ANY)
    sd = jax.ShapeDtypeStruct((1, hid, width), BF)
    return pl.pallas_call(
        grads_kernel,
        name="weight_grads",
        in_specs=[hbm] * 4,
        out_specs=[hbm] * 3,
        out_shape=[sd, sd, sd],
        scratch_shapes=[
            pltpu.VMEM((n, total, blk), BF),
            pltpu.VMEM((n, total, blk), BF),
            pltpu.VMEM((total, 1), F32),
            pltpu.VMEM((3, total, hid), BF),
            pltpu.VMEM((3, hid, total), BF),
            pltpu.VMEM((3, hid, width), BF),
            pltpu.SemaphoreType.DMA((2,)),
            pltpu.SemaphoreType.DMA((n,)),
            pltpu.SemaphoreType.DMA((n,)),
            pltpu.SemaphoreType.DMA((3,)),
        ],
        compiler_params=pltpu.CompilerParams(vmem_limit_bytes=60 * 2**20),
        interpret=INTERPRET,
    )(x_rows, d_rows, gate, acts)


def on_device(tokens, grad_out, gate_weight, up_weight, down_weight, gate_values, chosen, counts):
    y = lax.axis_index("y")
    z = lax.axis_index("z")
    c = lax.axis_index("c")
    x = lax.axis_index("x")
    ep = (y * NZ + z) * NC + c
    tok_rows, quarter = tokens.shape
    experts = chosen.shape[0]
    total = NZ * LINE
    part = quarter // NC
    half = NX * part
    plane = ("y", "c", "x")

    gw, uw, dw = gate_weight[0], up_weight[0], down_weight[0]

    onehot, px, pd = picks(tokens, grad_out, chosen, counts, ep)
    cut = part // 2
    send = jnp.stack([px, pd], 0).reshape(2, experts, SLOTS, NC, 2, cut)
    send = send.transpose(3, 1, 4, 0, 2, 5).reshape(1, NC * experts, 4 * SLOTS, cut)
    send = jnp.broadcast_to(send, (NY,) + send.shape[1:]).reshape(-1, 4 * SLOTS, cut)
    got = lax.all_to_all(send, plane, 0, 0, tiled=True)
    got = got.reshape(NY, NC, NX, 2, 2, SLOTS, cut).transpose(4, 0, 1, 5, 2, 3, 6)
    line = got.reshape(2 * LINE, half)

    hits = slot_table(
        lax.dynamic_index_in_dim(chosen, x, 0, keepdims=False),
        lax.dynamic_index_in_dim(counts, x, 0, keepdims=False),
        tok_rows,
        total,
        z,
    )
    gate = jnp.sum(jnp.where(hits, gate_values[0][None, :], 0.0), axis=1)[:, None]
    idx = c.astype(jnp.int32)[None]

    pieces = [line]
    up, dn = line, line
    for k in range(3):
        if k == 2:
            up, dn, gate = lax.optimization_barrier((up, dn, gate))
        up = lax.ppermute(up, "z", shift(NZ, 1))
        dn = lax.ppermute(dn, "z", shift(NZ, -1))
        pieces += [up, dn]
    pieces.append(lax.ppermute(up[:LINE], "z", shift(NZ, 1)))
    pieces.append(lax.ppermute(dn[LINE:], "z", shift(NZ, -1)))
    order = list(range(6, -1, -1))
    x_rows, d_rows, score, acts, far_away, away, far_home, home = forward(
        [(7, 0)] + [(k, 0) for k in order], [(8, 0)] + [(k, LINE) for k in order],
        idx, gate, gw, uw, dw, pieces, [swap(v) for v in pieces],
    )

    far_away, away = swap(far_away), swap(away)
    sums = jnp.split(far_away.astype(F32) + far_home, N_FAR, 0)
    sums += jnp.split(away.astype(F32) + home, N_NEAR, 0)
    score = jnp.sum(jnp.where(hits, score, 0.0), axis=0)
    hl = LINE // 2
    up, dn = sums[0][:hl].astype(BF), sums[0][hl:].astype(BF)
    for k, stage in enumerate((("y", NY, 2), ("y", NY, 1), ("z", NZ, 2), ("z", NZ, 4))):
        n = up.shape[0]
        up = lax.ppermute(up, "z", shift(NZ, 1)).astype(F32)
        dn = lax.ppermute(dn, "z", shift(NZ, -1)).astype(F32)
        score = pair_sum(score, *stage)
        if k < 3:
            if k == 0:
                up = jnp.pad(up, ((0, LINE - n), (0, 0)))
                dn = jnp.pad(dn, ((LINE - n, 0), (0, 0)))
            up, dn = sums[2 * k + 1] + up, sums[2 * k + 2] + dn
            up, dn = up.astype(BF), dn.astype(BF)
            if k < 2:
                up, dn, score = lax.optimization_barrier((up, dn, score))
            else:
                up, dn, score, acts = lax.optimization_barrier((up, dn, score, acts))
    rows = (sums[7] + up + dn).astype(BF)
    grad_g, grad_u, grad_d = grads(x_rows, d_rows, gate, acts, part)
    rows, grad_g, grad_u, grad_d, score = lax.optimization_barrier(
        (rows, grad_g, grad_u, grad_d, score)
    )
    score = pair_sum(pair_sum(score, "z", NZ, 1), "c", NC, 1)

    cut = part // 4
    back = rows.reshape(NY, NC, SLOTS, NX, 4, cut).transpose(0, 1, 3, 4, 2, 5)
    back = lax.all_to_all(back.reshape(-1, 4 * SLOTS, cut), plane, 0, 0, tiled=True)
    back = jnp.sum(back.reshape(NY, NC, experts, 4, SLOTS, cut).astype(F32), 0)
    back = back.transpose(1, 3, 0, 2, 4).reshape(experts * SLOTS, quarter)
    tn = (((0,), (0,)), ((), ()))
    token_grad = lax.dot_general(
        onehot.astype(F32), back, tn, precision=lax.Precision.HIGHEST, preferred_element_type=F32
    ).astype(BF)
    return grad_g, grad_u, grad_d, token_grad, score[None]


def solution(mesh):
    torus = Mesh(mesh.devices.reshape(NY, NZ, NC, NX), ("y", "z", "c", "x"))
    ep = ("y", "z", "c")
    return jax.shard_map(
        on_device,
        mesh=torus,
        in_specs=(
            P(ep, "x"),
            P(ep, "x"),
            P("x", ep, None),
            P("x", ep, None),
            P("x", ep, None),
            P("x", None),
            P(),
            P(),
        ),
        out_specs=(
            P("x", ep, None),
            P("x", ep, None),
            P("x", ep, None),
            P(ep, "x"),
            P("x", None),
        ),
        check_vma=False,
    )
```

```python
import functools

import jax
import jax.numpy as jnp
from jax import lax
from jax.experimental import pallas as pl
from jax.experimental.pallas import tpu as pltpu
from jax.sharding import Mesh
from jax.sharding import PartitionSpec as P

SLOTS = 6
NY, NZ, NC, NX = 4, 8, 2, 4
BF, F32 = jnp.bfloat16, jnp.float32
INTERPRET = False
NT = (((1,), (1,)), ((), ()))


def shift(n, s):
    return [(i, (i + s) % n) for i in range(n)]


def swap(v):
    return lax.ppermute(v, "c", [(0, 1), (1, 0)])


def pair_sum(v, axis, n, step):
    return v + lax.ppermute(v, axis, [(i, i ^ step) for i in range(n)])


def picks(tokens, grad_out, chosen, counts, ep):
    cap = chosen.shape[1]
    tok_rows = tokens.shape[0]
    col = lax.broadcasted_iota(jnp.int32, chosen.shape, 1)
    mine = (col < counts[:, None]) & (chosen // tok_rows == ep)
    before = lax.broadcasted_iota(jnp.int32, (cap, cap), 0) < lax.broadcasted_iota(
        jnp.int32, (cap, cap), 1
    )
    rank = jnp.dot(mine.astype(BF), before.astype(BF), preferred_element_type=F32).astype(jnp.int32)
    slot = lax.broadcasted_iota(jnp.int32, (1, SLOTS, 1), 1)
    hit = mine[:, None, :] & (rank[:, None, :] == slot)
    row = jnp.sum(jnp.where(hit, (chosen - ep * tok_rows)[:, None, :] + 1, 0), axis=2) - 1
    row = row.reshape(-1)
    onehot = (row[:, None] == lax.broadcasted_iota(jnp.int32, (1, tok_rows), 1)).astype(BF)
    px = jnp.dot(onehot, tokens, preferred_element_type=F32).astype(BF)
    pd = jnp.dot(onehot, grad_out, preferred_element_type=F32).astype(BF)
    return onehot, px, pd


def slot_table(chosen_e, count_e, tok_rows, total, z):
    cap = chosen_e.shape[0]
    col = lax.broadcasted_iota(jnp.int32, (cap,), 0)
    live = col < count_e
    block = jnp.where(live, chosen_e // tok_rows, -1)
    same = (block[:, None] == block[None, :]) & (col[:, None] < col[None, :])
    rank = jnp.sum(same.astype(jnp.int32), axis=0)
    rel = (block // NC - z) % NZ
    line = jnp.where(rel < 4, 7 - 2 * rel, 2 * rel - 8)
    pos = ((line * NY + block // (NC * NZ)) * NC + block % NC) * SLOTS + rank
    pos = jnp.where(live, pos, total)
    return pos == lax.broadcasted_iota(jnp.int32, (total, cap), 0)


LINE = NY * NC * SLOTS
N_NEAR, N_FAR = 5, 3


def forward_kernel(x_src, d_src, idx, gate, gw, uw, dw, *refs):
    n = (len(refs) - 14) // 2
    mine, other = refs[:n], refs[n : 2 * n]
    x_out, d_out, score, acts, far_away, away, far_home, home = refs[2 * n : 2 * n + 8]
    xv, dv, gv, uv, wv, sem = refs[2 * n + 8 :]
    c = idx[0]
    half = xv.shape[2]
    part = half // NX

    def place(sources, dst, s):
        for i, (k, first) in enumerate(sources):
            for src, h in ((mine[k], c), (other[k], 1 - c)):
                pltpu.make_async_copy(
                    src.at[pl.ds(first, LINE), :], dst.at[h, pl.ds(i * LINE, LINE), :], sem.at[s]
                ).start()

    def weight(w, v, s):
        for q in range(NX):
            for h in range(NC):
                pltpu.make_async_copy(
                    w.at[:, pl.ds((q * NC + h) * part, part)],
                    v.at[h, :, pl.ds(q * part, part)],
                    sem.at[s],
                ).start()

    place(x_src, xv, 0)
    weight(gw, gv, 2)
    weight(uw, uv, 3)
    place(d_src, dv, 1)
    weight(dw, wv, 4)

    def landed(v, s):
        pltpu.make_async_copy(v, v, sem.at[s]).wait()

    def product(a, w):
        def add(h, acc):
            return acc + lax.dot_general(a[h], w[h], NT, preferred_element_type=F32)

        return lax.fori_loop(0, NC, add, jnp.zeros((a.shape[1], w.shape[1]), F32))

    landed(xv, 0)
    keep_x = pltpu.make_async_copy(xv, x_out, sem.at[5])
    keep_x.start()
    landed(gv, 2)
    pre_gate = product(xv, gv)
    landed(uv, 3)
    pre_up = product(xv, uv)
    landed(dv, 1)
    keep_d = pltpu.make_async_copy(dv, d_out, sem.at[6])
    keep_d.start()
    landed(wv, 4)
    probe = product(dv, wv)
    sig = jax.nn.sigmoid(pre_gate)
    swished = pre_gate * sig
    active = (swished * pre_up).astype(BF)
    score[...] = jnp.sum(active.astype(F32) * probe, axis=1, keepdims=True)
    d_active = gate[...] * probe
    d_gate = (d_active * pre_up * sig * (1.0 + pre_gate * (1.0 - sig))).astype(BF)
    d_up = (d_active * swished).astype(BF)
    acts[0] = d_gate
    acts[1] = d_up
    acts[2] = active

    cut = far_away.shape[0]
    for h, far, near in ((1 - c, far_away, away), (c, far_home, home)):
        for q in range(NX):
            cols = pl.ds(q * part, part)
            r = jnp.dot(d_gate, gv[h, :, cols], preferred_element_type=F32)
            r += jnp.dot(d_up, uv[h, :, cols], preferred_element_type=F32)
            r = r.astype(far.dtype)
            far[:, cols] = r[:cut]
            near[:, cols] = r[cut:]
    keep_x.wait()
    keep_d.wait()


def forward(x_src, d_src, idx, gate, gw, uw, dw, pieces, swapped):
    hid = gw.shape[0]
    rows = gate.shape[0]
    half = pieces[0].shape[1]
    vm = pl.BlockSpec(memory_space=pltpu.VMEM)
    hbm = pl.BlockSpec(memory_space=pl.ANY)
    sd = jax.ShapeDtypeStruct
    return pl.pallas_call(
        functools.partial(forward_kernel, x_src, d_src),
        name="forward",
        in_specs=[pl.BlockSpec(memory_space=pltpu.SMEM), vm] + [hbm] * (3 + 2 * len(pieces)),
        out_specs=[hbm, hbm] + [vm] * 6,
        out_shape=[
            sd((NC, rows, half), BF),
            sd((NC, rows, half), BF),
            sd((rows, 1), F32),
            sd((3, rows, hid), BF),
            sd((N_FAR * LINE, half), BF),
            sd((N_NEAR * LINE, half), BF),
            sd((N_FAR * LINE, half), F32),
            sd((N_NEAR * LINE, half), F32),
        ],
        scratch_shapes=[
            pltpu.VMEM((NC, rows, half), BF),
            pltpu.VMEM((NC, rows, half), BF),
            pltpu.VMEM((NC, hid, half), BF),
            pltpu.VMEM((NC, hid, half), BF),
            pltpu.VMEM((NC, hid, half), BF),
            pltpu.SemaphoreType.DMA((7,)),
        ],
        compiler_params=pltpu.CompilerParams(vmem_limit_bytes=60 * 2**20),
        interpret=INTERPRET,
    )(idx, gate, gw, uw, dw, *pieces, *swapped)


def grads_kernel(first, weigh, rows, gate, acts, *refs):
    count = len(refs) - 8
    outs = refs[:count]
    xv, gate_v, av, tv, ov, sem, sem_x, sem_o = refs[count:]
    n, total, blk = xv.shape
    small = (
        pltpu.make_async_copy(acts.at[pl.ds(first, count)], av, sem.at[0]),
        pltpu.make_async_copy(gate, gate_v, sem.at[1]),
    )
    for v in small:
        v.start()

    def block(k):
        cols = pl.ds(pl.multiple_of(k // NC * blk, blk), blk)
        return pltpu.make_async_copy(rows.at[lax.rem(k, NC), :, cols], xv.at[k], sem_x.at[k])

    @pl.loop(0, n)
    def _(k):
        block(k).start()

    for v in small:
        v.wait()
    for t in range(count):
        tv[t] = av[t].astype(F32).T.astype(BF)

    @pl.loop(0, n)
    def _(k):
        cols = pl.ds(pl.multiple_of(k * blk, blk), blk)
        block(k).wait()
        rhs = xv[k]
        if weigh:
            rhs = (gate_v[...] * rhs.astype(F32)).astype(BF)
        for t, dst in enumerate(outs):
            ov[t, :, cols] = jnp.dot(tv[t], rhs, preferred_element_type=F32).astype(BF)
            pltpu.make_async_copy(ov.at[t, :, cols], dst.at[0, :, cols], sem_o.at[t]).start()

    for t, dst in enumerate(outs):
        pltpu.make_async_copy(ov.at[t], dst.at[0], sem_o.at[t]).wait()


def grads(first, count, weigh, rows, gate, acts, blk):
    _, total, hid = acts.shape
    width = NC * rows.shape[2]
    n = width // blk
    hbm = pl.BlockSpec(memory_space=pl.ANY)
    sd = jax.ShapeDtypeStruct((1, hid, width), BF)
    return pl.pallas_call(
        functools.partial(grads_kernel, first, weigh),
        name="down_grads" if weigh else "gate_up_grads",
        in_specs=[hbm] * 3,
        out_specs=[hbm] * count,
        out_shape=[sd] * count,
        scratch_shapes=[
            pltpu.VMEM((n, total, blk), BF),
            pltpu.VMEM((total, 1), F32),
            pltpu.VMEM((count, total, hid), BF),
            pltpu.VMEM((count, hid, total), BF),
            pltpu.VMEM((count, hid, width), BF),
            pltpu.SemaphoreType.DMA((2,)),
            pltpu.SemaphoreType.DMA((n,)),
            pltpu.SemaphoreType.DMA((count,)),
        ],
        compiler_params=pltpu.CompilerParams(vmem_limit_bytes=60 * 2**20),
        interpret=INTERPRET,
    )(rows, gate, acts)


def on_device(tokens, grad_out, gate_weight, up_weight, down_weight, gate_values, chosen, counts):
    y = lax.axis_index("y")
    z = lax.axis_index("z")
    c = lax.axis_index("c")
    x = lax.axis_index("x")
    ep = (y * NZ + z) * NC + c
    tok_rows, quarter = tokens.shape
    experts = chosen.shape[0]
    total = NZ * LINE
    part = quarter // NC
    half = NX * part
    plane = ("y", "c", "x")

    gw, uw, dw = gate_weight[0], up_weight[0], down_weight[0]

    onehot, px, pd = picks(tokens, grad_out, chosen, counts, ep)
    cut = part // 2
    send = jnp.stack([px, pd], 0).reshape(2, experts, SLOTS, NC, 2, cut)
    send = send.transpose(3, 1, 4, 0, 2, 5).reshape(1, NC * experts, 4 * SLOTS, cut)
    send = jnp.broadcast_to(send, (NY,) + send.shape[1:]).reshape(-1, 4 * SLOTS, cut)
    got = lax.all_to_all(send, plane, 0, 0, tiled=True)
    got = got.reshape(NY, NC, NX, 2, 2, SLOTS, cut).transpose(4, 0, 1, 5, 2, 3, 6)
    line = got.reshape(2 * LINE, half)

    hits = slot_table(
        lax.dynamic_index_in_dim(chosen, x, 0, keepdims=False),
        lax.dynamic_index_in_dim(counts, x, 0, keepdims=False),
        tok_rows,
        total,
        z,
    )
    gate = jnp.sum(jnp.where(hits, gate_values[0][None, :], 0.0), axis=1)[:, None]
    idx = c.astype(jnp.int32)[None]

    pieces = [line]
    up, dn = line, line
    for k in range(3):
        if k == 2:
            up, dn, gate = lax.optimization_barrier((up, dn, gate))
        up = lax.ppermute(up, "z", shift(NZ, 1))
        dn = lax.ppermute(dn, "z", shift(NZ, -1))
        pieces += [up, dn]
    pieces.append(lax.ppermute(up[:LINE], "z", shift(NZ, 1)))
    pieces.append(lax.ppermute(dn[LINE:], "z", shift(NZ, -1)))
    order = list(range(6, -1, -1))
    x_rows, d_rows, score, acts, far_away, away, far_home, home = forward(
        [(7, 0)] + [(k, 0) for k in order], [(8, 0)] + [(k, LINE) for k in order],
        idx, gate, gw, uw, dw, pieces, [swap(v) for v in pieces],
    )

    far_away, away = swap(far_away), swap(away)
    sums = jnp.split(far_away.astype(F32) + far_home, N_FAR, 0)
    sums += jnp.split(away.astype(F32) + home, N_NEAR, 0)
    score = jnp.sum(jnp.where(hits, score, 0.0), axis=0)
    hl = LINE // 2
    up, dn = sums[0][:hl].astype(BF), sums[0][hl:].astype(BF)
    for k, stage in enumerate((("y", NY, 2), ("y", NY, 1), ("z", NZ, 2), ("z", NZ, 4))):
        n = up.shape[0]
        up = lax.ppermute(up, "z", shift(NZ, 1)).astype(F32)
        dn = lax.ppermute(dn, "z", shift(NZ, -1)).astype(F32)
        score = pair_sum(score, *stage)
        if k < 3:
            if k == 0:
                up = jnp.pad(up, ((0, LINE - n), (0, 0)))
                dn = jnp.pad(dn, ((LINE - n, 0), (0, 0)))
            up, dn = sums[2 * k + 1] + up, sums[2 * k + 2] + dn
            up, dn = up.astype(BF), dn.astype(BF)
            if k < 2:
                up, dn, score = lax.optimization_barrier((up, dn, score))
            else:
                up, dn, score, acts = lax.optimization_barrier((up, dn, score, acts))
    rows = (sums[7] + up + dn).astype(BF)
    grad_g, grad_u = grads(0, 2, False, x_rows, gate, acts, part)
    rows, grad_g, grad_u, score, acts = lax.optimization_barrier(
        (rows, grad_g, grad_u, score, acts)
    )
    (grad_d,) = grads(2, 1, True, d_rows, gate, acts, part)
    score = pair_sum(pair_sum(score, "z", NZ, 1), "c", NC, 1)

    cut = part // 4
    back = rows.reshape(NY, NC, SLOTS, NX, 4, cut).transpose(0, 1, 3, 4, 2, 5)
    back = lax.all_to_all(back.reshape(-1, 4 * SLOTS, cut), plane, 0, 0, tiled=True)
    back = jnp.sum(back.reshape(NY, NC, experts, 4, SLOTS, cut).astype(F32), 0)
    back = back.transpose(1, 3, 0, 2, 4).reshape(experts * SLOTS, quarter)
    tn = (((0,), (0,)), ((), ()))
    token_grad = lax.dot_general(
        onehot.astype(F32), back, tn, precision=lax.Precision.HIGHEST, preferred_element_type=F32
    ).astype(BF)
    return grad_g, grad_u, grad_d, token_grad, score[None]


def solution(mesh):
    torus = Mesh(mesh.devices.reshape(NY, NZ, NC, NX), ("y", "z", "c", "x"))
    ep = ("y", "z", "c")
    return jax.shard_map(
        on_device,
        mesh=torus,
        in_specs=(
            P(ep, "x"),
            P(ep, "x"),
            P("x", ep, None),
            P("x", ep, None),
            P("x", ep, None),
            P("x", None),
            P(),
            P(),
        ),
        out_specs=(
            P("x", ep, None),
            P("x", ep, None),
            P("x", ep, None),
            P(ep, "x"),
            P("x", None),
        ),
        check_vma=False,
    )
```
